32 devices in a mesh: dp: 16 (over z, y, core), owner: 2 (over x).
Axes of the slice: x: 2, y: 2, z: 4, core: 2. Of those that a mesh axis runs over, the one named last changes fastest.
Arguments:
- hidden: bfloat16 [2048, 4096], P('dp'), may hold values from -6 to 6
- norm_gain: float32 [4096], replicated, may hold values from 0.3 to 3
- cotangent: bfloat16 [2048, 6144], P('dp'), may hold values from -30 to 30
Outputs:
- update: bfloat16 [6144, 4096], P('dp', 'owner')
The draws below stay inside these ranges and needn't reach their ends.
All inputs are finite; a program needn't handle non-finite values. Where the reference program divides by a largest or mean magnitude, that divisor is 1e-20 or more.
Results may differ from the reference program's by a relative error of at most 0.014.
Values may be sent and summed in bfloat16 or wider, within the bound.
A program may use at most 128 MiB of HBM per device.

```python
import math
import jax
import jax.numpy as jnp
from jax import lax

D = 4096
TILE = 1024
TOK_DEV = 128
TOKENS = 2048
DOUT = 6144
NBLK = 10
N_DP = 16


latent_rank = 16


def shared_latent(key):
    return jax.random.normal(jax.random.fold_in(key, 5), (TOKENS, latent_rank), jnp.float32)


def draw_hidden(key, part):
    latent = shared_latent(key)
    keys = jax.random.split(jax.random.fold_in(key, 23), 2)
    basis = jax.random.normal(keys[0], (latent_rank, D), jnp.float32) / math.sqrt(latent_rank)
    noise = jax.random.normal(keys[1], (TOKENS, D), jnp.float32)
    share = 0.5
    mixed = jnp.dot(latent, basis)
    values = math.sqrt(1.0 - share * share) * noise + share * mixed
    return jnp.clip(values, -6.0, 6.0).astype(jnp.bfloat16)


def draw_cotangent(key, part):
    latent = shared_latent(key)
    keys = jax.random.split(jax.random.fold_in(key, 17), 8)
    columns = 3.0 ** (jnp.arange(DOUT, dtype=jnp.float32) / DOUT)
    columns = columns * jax.random.uniform(keys[1], (DOUT,), jnp.float32, 0.5, 1.5)
    heavy = jax.random.randint(keys[4], (), 0, N_DP)
    group_index = jnp.arange(TOKENS, dtype=jnp.int32) // TOK_DEV
    before = (heavy + N_DP - 1) % N_DP
    chosen = jnp.logical_or(group_index == heavy, group_index == before)
    group_scale = jnp.where(chosen, 5.0, 1.0).astype(jnp.float32)[:, None]
    common_basis = jax.random.normal(keys[5], (latent_rank, DOUT), jnp.float32) / math.sqrt(latent_rank)
    own_basis = jax.random.normal(keys[6], (N_DP, latent_rank, DOUT), jnp.float32) / math.sqrt(latent_rank)
    own_latent = jax.random.normal(keys[7], (N_DP, TOK_DEV, latent_rank), jnp.float32)
    own = jnp.einsum('gtr,grc->gtc', own_latent, own_basis).reshape(TOKENS, DOUT)
    common = jnp.dot(latent, common_basis)
    noise = jax.random.normal(keys[0], (TOKENS, DOUT), jnp.float32)
    noise_share = 0.6
    common_share = 0.4
    own_share = math.sqrt(1.0 - noise_share * noise_share - common_share * common_share)
    values = noise_share * noise + common_share * common + own_share * own
    values = values * group_scale
    return jnp.clip(values * columns, -30.0, 30.0).astype(jnp.bfloat16)


def setup_inputs(seed: int = 0) -> dict:
    arg_keys = jax.random.split(jax.random.key(seed), 4)
    hidden = draw_hidden(jax.random.fold_in(arg_keys[3], 71), 0)
    norm_gain = jnp.clip(jnp.exp(jax.random.uniform(arg_keys[1], (D,), jnp.float32, math.log(0.3), math.log(3.0))), 0.3, 3.0)
    cotangent = draw_cotangent(jax.random.fold_in(arg_keys[3], 71), 0)
    return {"hidden": hidden, "norm_gain": norm_gain, "cotangent": cotangent}


DAMPING = 0.1

def rounded(value):
    return lax.optimization_barrier(value.astype(jnp.bfloat16)).astype(jnp.float32)

def reference(hidden, norm_gain, cotangent):
    highest = lax.Precision.HIGHEST
    states = hidden.astype(jnp.float32)
    normed = (states * lax.rsqrt(lax.optimization_barrier(jnp.mean(states * states, axis=1, keepdims=True)) + 1e-05) * norm_gain).astype(jnp.bfloat16)
    source = jnp.concatenate([normed, cotangent], axis=1)
    identity = jnp.eye(TILE, dtype=jnp.float32)
    results = []
    for block in range(NBLK):
        piece = source[:, block * TILE:(block + 1) * TILE].astype(jnp.float32)
        factor = jnp.dot(piece.T, piece, precision=highest)
        matrix = factor / TOKENS + DAMPING * identity
        scale = 1.0 / jnp.max(lax.optimization_barrier(jnp.sum(jnp.abs(matrix), axis=1)))
        first = 2.0 * scale * identity - scale * scale * matrix
        first_low = rounded(first)
        product = rounded(jnp.dot(first_low, rounded(matrix), precision=highest))
        inverse = rounded(2.0 * first - jnp.dot(product, first_low, precision=highest))
        results.append(jnp.dot(piece, inverse, precision=highest).astype(jnp.bfloat16))
    inputs_side = D // TILE
    pre_in = jnp.concatenate(results[:inputs_side], axis=1).astype(jnp.float32).reshape(N_DP, TOK_DEV, D)
    pre_out = jnp.concatenate(results[inputs_side:], axis=1).astype(jnp.float32).reshape(N_DP, TOK_DEV, DOUT)

    def accumulate(total, pair):
        left, right = pair
        return (total + rounded(jnp.dot(right.T, left, precision=highest)), None)
    summed, _ = lax.scan(accumulate, jnp.zeros((DOUT, D), jnp.float32), (pre_in, pre_out))
    squares = jnp.sum(summed * summed)
    return (summed * lax.rsqrt(squares / (D * DOUT) + 1e-06)).astype(jnp.bfloat16)
```

```python
import functools

import jax
import jax.numpy as jnp
from jax import lax
from jax.experimental import pallas as pl
from jax.experimental.pallas import tpu as pltpu
from jax.sharding import PartitionSpec as P

TILE = 1024


DAMPING = 0.1


def contract(left, right, left_dim, right_dim):
    return lax.dot_general(
        left, right, (((left_dim,), (right_dim,)), ((), ())), preferred_element_type=jnp.float32
    )


def inverse_of(piece, tokens):
    identity = jnp.eye(TILE, dtype=jnp.float32)
    matrix = contract(piece, piece, 0, 0) / tokens + DAMPING * identity
    scale = 1.0 / jnp.max(jnp.sum(jnp.abs(matrix), axis=1))
    first = 2.0 * scale * identity - (scale * scale) * matrix
    first_low = first.astype(jnp.bfloat16)
    matrix_low = matrix.astype(jnp.bfloat16)
    product = contract(first_low, matrix_low, 1, 0).astype(jnp.bfloat16)
    return (2.0 * first - contract(product, first_low, 1, 0)).astype(jnp.bfloat16)


def shards(hidden, norm_gain, cotangent):
    owners = lax.axis_size("owner")
    position = lax.axis_index("owner")
    groups = lax.axis_size("dp")
    group = lax.axis_index("dp")
    tokens_here = hidden.shape[0]
    tokens = tokens_here * groups
    width = hidden.shape[1]
    out_width = cotangent.shape[1]
    strip = out_width // groups
    own = width // owners
    in_width = max(own, TILE)

    firsts = jnp.array([(g * strip) // TILE for g in range(groups)], jnp.int32)
    lasts = jnp.array([((g + 1) * strip - 1) // TILE for g in range(groups)], jnp.int32)
    odd = lax.rem(position, 2) == 1
    wanted = jnp.where(odd, lasts, firsts)
    outgoing = jnp.stack(
        [
            lax.dynamic_slice_in_dim(cotangent, wanted[g] * TILE, TILE, 1)
            for g in range(groups)
        ]
    )
    out_piece = lax.all_to_all(outgoing, "dp", 0, 0, tiled=True).reshape(tokens, TILE)

    states = hidden.astype(jnp.float32)
    normed = (
        states * lax.rsqrt(jnp.mean(states * states, axis=1, keepdims=True) + 1e-05) * norm_gain
    ).astype(jnp.bfloat16)
    in_start = (position * own) // TILE * TILE
    mine = lax.dynamic_slice_in_dim(normed, in_start, in_width, 1)
    in_piece = lax.all_gather(mine, "dp", axis=0, tiled=True)

    out_inverse = inverse_of(out_piece, tokens)
    padded = jnp.pad(out_inverse, ((0, 0), (strip, strip)))
    offset = group * strip - wanted[group] * TILE
    strip_inverse = lax.dynamic_slice_in_dim(padded, offset + strip, strip, 1)
    part = contract(out_piece, strip_inverse, 1, 0).astype(jnp.bfloat16)
    other = lax.ppermute(part, "owner", [(o, o ^ 1) for o in range(owners)])
    column_block = (group * strip + jnp.arange(strip, dtype=jnp.int32)) // TILE
    pre_out = jnp.where((column_block == wanted[group])[None, :], part, other)

    results = []
    for block in range(in_width // TILE):
        piece = in_piece[:, block * TILE : (block + 1) * TILE]
        inverse = inverse_of(piece, tokens)
        if own < TILE:
            inverse = lax.dynamic_slice_in_dim(inverse, position * own - in_start, own, 1)
        cross = contract(pre_out, piece, 0, 0).astype(jnp.bfloat16)
        results.append(contract(cross, inverse, 1, 0))
    summed = jnp.concatenate(results, axis=1)
    squares = lax.psum(jnp.sum(summed * summed), ("dp", "owner"))
    return (summed * lax.rsqrt(squares / (width * out_width) + 1e-06)).astype(jnp.bfloat16)


MESH = pl.DeviceIdType.MESH
UNIT = TILE // 4
CHUNK = 128


def flipped(value, mask):
    for bit in range(mask.bit_length()):
        if (mask >> bit) & 1:
            value = value + (1 - 2 * ((value // 2**bit) % 2)) * 2**bit
    return value


def matrix_chunk(gram, tokens, i):
    shape = (CHUNK, TILE)
    row = lax.broadcasted_iota(jnp.int32, shape, 0) + i * CHUNK
    column = lax.broadcasted_iota(jnp.int32, shape, 1)
    rows = pl.ds(pl.multiple_of(i * CHUNK, CHUNK), CHUNK)
    return gram[rows, :] * (1.0 / tokens) + jnp.where(row == column, DAMPING, 0.0)


def scaled_factor(gram, low, tokens):
    def add(i, total):
        return total + jnp.sum(jnp.abs(matrix_chunk(gram, tokens, i)), axis=0, keepdims=True)

    sums = lax.fori_loop(0, TILE // CHUNK, add, jnp.zeros((1, TILE), jnp.float32))
    scale = 1.0 / jnp.max(sums, axis=1, keepdims=True)

    def put(i, carry):
        rows = pl.ds(pl.multiple_of(i * CHUNK, CHUNK), CHUNK)
        low[rows, :] = (scale * matrix_chunk(gram, tokens, i)).astype(jnp.bfloat16)
        return carry

    lax.fori_loop(0, TILE // CHUNK, put, 0)
    return scale


def whole_kernel(
    sizes,
    hidden_ref,
    gain_ref,
    cotangent_ref,
    update_ref,
    states,
    cbuf,
    nbuf,
    other_n,
    gram_c,
    gram_n,
    low_c,
    low_n,
    pre,
    give,
    cross,
    mine,
    theirs,
    arrived,
    squares,
    load_sem,
    c_send,
    c_x,
    c_core,
    c_recv,
    n_core,
    n_up,
    n_down,
    n_y,
    n_recv,
    pre_send,
    pre_recv,
    swap_send,
    swap_recv,
    sq_send,
    sq_recv,
):
    groups, owners, tokens_here, width, out_width = sizes
    tokens = groups * tokens_here
    line = groups // 4
    strip = out_width // groups
    own = width // owners
    me = lax.axis_index("dp")
    x = lax.axis_index("owner")
    z = me // 4
    y = (me // 2) % 2
    c = me % 2
    devices = groups * owners
    flat = me * owners + x

    def slot_of(y_, z_, c_):
        return (y_ * line + z_) * 2 + c_

    def device(x_, y_, z_, c_):
        return ((z_ * 2 + y_) * 2 + c_, x_)

    def block_of(p):
        return 3 * (p // 4) + (p % 4 + 1) // 2

    def remote(src, dst, send, recv, target):
        return pltpu.make_async_remote_copy(
            src_ref=src,
            dst_ref=dst,
            send_sem=send,
            recv_sem=recv,
            device_id=target,
            device_id_type=MESH,
        )

    own_slot = slot_of(y, z, c)
    core_slot = slot_of(y, z, 1 - c)
    core_peer = device(x, y, z, 1 - c)
    x_peer = device(1 - x, y, z, c)

    load = pltpu.make_async_copy(hidden_ref, states, load_sem.at[0])
    load.start()

    barrier = pltpu.get_barrier_semaphore()

    def greet(d, carry):
        target = (flat + d) % devices
        pl.semaphore_signal(
            barrier, inc=1, device_id=(target // owners, target % owners), device_id_type=MESH
        )
        return carry

    lax.fori_loop(1, devices, greet, 0)
    pl.semaphore_wait(barrier, devices - 1)

    def block_columns(y_, z_):
        return pl.ds(pl.multiple_of(block_of(z_ * 2 + y_) * TILE, TILE), TILE)

    def c_out(k):
        zd = flipped(z, k)
        yd = (y + x + z + zd) % 2
        return remote(
            cotangent_ref.at[:, block_columns(yd, zd)],
            cbuf.at[own_slot],
            c_send.at[k],
            c_recv.at[own_slot],
            device(x, yd, zd, c),
        )

    def c_in_slot(k, through):
        zs = flipped(z, k)
        ys = (y + x + through + z + zs) % 2
        return slot_of(ys, zs, c)

    def c_relay(slot, sems, target):
        return remote(cbuf.at[slot], cbuf.at[slot], sems.at[slot], c_recv.at[slot], target)

    for k in range(1, line):
        c_out(k).start()

    @pl.when(x == 1)
    def _():
        c_out(0).start()

    local = pltpu.make_async_copy(
        cotangent_ref.at[:, block_columns(y, z)], cbuf.at[own_slot], load_sem.at[1]
    )
    local.start()
    c_own = remote(
        cotangent_ref.at[:, block_columns(y, z)],
        cbuf.at[own_slot],
        c_core.at[own_slot],
        c_recv.at[own_slot],
        core_peer,
    )
    c_own.start()

    load.wait()
    part = 16
    kept = pl.ds(pl.multiple_of(x * own + c * TILE, TILE), TILE)
    passed = pl.ds(pl.multiple_of(x * own + (1 - c) * TILE, TILE), TILE)

    def normalize(i, carry):
        rows = pl.ds(pl.multiple_of(i * part, part), part)
        full = states[rows, :].astype(jnp.float32)
        factor = lax.rsqrt(jnp.sum(full * full, axis=1, keepdims=True) * (1.0 / width) + 1e-05)
        for columns, put in ((passed, other_n), (kept, nbuf.at[own_slot])):
            piece = states[rows, columns].astype(jnp.float32) * factor * gain_ref[:, columns]
            put[rows, :] = piece.astype(jnp.bfloat16)
        return carry

    lax.fori_loop(0, tokens_here // part, normalize, 0)
    n_pass = remote(other_n, nbuf.at[own_slot], n_core.at[0], n_recv.at[own_slot], core_peer)
    n_pass.start()

    def n_copy(slot, sems, target):
        return remote(nbuf.at[slot], nbuf.at[slot], sems.at[slot], n_recv.at[slot], target)

    def n_to_y(slot):
        return n_copy(slot, n_y, device(x, 1 - y, z, c))

    def n_to_up(slot):
        return n_copy(slot, n_up, device(x, y, z + 1, c))

    def n_to_down(slot):
        return n_copy(slot, n_down, device(x, y, z - 1, c))

    def own_out(slot, act):
        act(n_to_y(slot))

        @pl.when(z + 1 < line)
        def _():
            act(n_to_up(slot))

        @pl.when(z > 0)
        def _():
            act(n_to_down(slot))

    def start(copy):
        copy.start()

    def drain(copy):
        copy.wait_send()

    own_out(own_slot, start)
    n_to_y(core_slot).wait_recv()
    own_out(core_slot, start)

    def line_source(i):
        low = jnp.minimum(z, line - 1 - z)
        near = i < 2 * low
        distance = jnp.where(near, i // 2 + 1, i + 1 - low)
        below = jnp.where(near, i % 2 == 0, z > low)
        return jnp.where(below, z - distance, z + distance), below

    def line_out(slot, below, act):
        act(n_to_y(slot))

        @pl.when(jnp.logical_and(below, z + 1 < line))
        def _():
            act(n_to_up(slot))

        @pl.when(jnp.logical_and(jnp.logical_not(below), z > 0))
        def _():
            act(n_to_down(slot))

    def line_step(i, carry):
        zs, below = line_source(i)
        for cs in range(2):
            slot = slot_of(y, zs, cs)
            n_to_y(slot).wait_recv()
            line_out(slot, below, start)
        return carry

    def c_direct(k):
        slot = c_in_slot(k, 0)
        c_relay(slot, c_x, x_peer).wait_recv()
        c_relay(slot, c_x, x_peer).start()
        c_relay(slot, c_core, core_peer).start()

    for k in range(1, line):
        c_direct(k)

    @pl.when(x == 1)
    def _():
        c_direct(0)

    line_step(0, 0)

    def c_shared(k):
        slot = c_in_slot(k, 1)
        c_relay(slot, c_core, core_peer).wait_recv()
        c_relay(slot, c_core, core_peer).start()

    for k in range(1, line):
        c_shared(k)

    @pl.when(x == 0)
    def _():
        c_shared(0)

    def c_from_core(i, carry):
        slot = 2 * i + 1 - c
        c_relay(slot, c_core, core_peer).wait_recv()
        return carry

    lax.fori_loop(0, groups // 2, c_from_core, 0)
    local.wait()

    line_step(1, 0)
    block_tokens = cbuf[...].reshape(tokens, TILE)
    gram_c[...] = contract(block_tokens, block_tokens, 0, 0)
    scale_c = scaled_factor(gram_c, low_c, tokens)
    lax.fori_loop(2, line - 1, line_step, 0)

    p = z * 2 + y
    r = p % 4
    edge = jnp.where(jnp.logical_or(r == 0, r == 3), 1, 0)
    block = block_of(p)

    def unit_of(k):
        return edge * (3 * c + k * (1 - 2 * c)) + (1 - edge) * (2 * (r - 1) + c)

    def place_of(k):
        return 4 * block + unit_of(k) - 3 * p

    def strip_columns(place):
        return pl.ds(pl.multiple_of(place * UNIT, UNIT), UNIT)

    def pre_copy(place, send, target):
        view = pre.at[:, strip_columns(place)]
        return remote(view, view, send, pre_recv.at[place], target)

    def give_copy(k):
        place = place_of(k) - 3 * (1 - 2 * y)
        return remote(
            give,
            pre.at[:, strip_columns(place)],
            pre_send.at[2],
            pre_recv.at[place],
            device(x, 1 - y, z, c),
        )

    def unit_value(k):
        unit = unit_of(k)
        first = low_c[:, pl.ds(pl.multiple_of(unit * UNIT, UNIT), UNIT)]
        second = contract(low_c[...], first, 1, 0)
        third = contract(low_c[...], second.astype(jnp.bfloat16), 1, 0)
        row = lax.broadcasted_iota(jnp.int32, (TILE, UNIT), 0)
        column = lax.broadcasted_iota(jnp.int32, (TILE, UNIT), 1) + unit * UNIT
        start4 = jnp.where(row == column, 4.0, 0.0)
        inverse = scale_c * (start4 - 6.0 * first.astype(jnp.float32) + 4.0 * second - third)
        whole = cbuf[...].reshape(tokens, TILE)
        return contract(whole, inverse.astype(jnp.bfloat16), 1, 0).astype(jnp.bfloat16)

    def is_mine(k):
        place = place_of(k)
        return jnp.logical_and(place >= 0, place < 3)

    def unit_step(k, carry):
        value = unit_value(k)
        inside = is_mine(k)

        @pl.when(inside)
        def _():
            pre[:, strip_columns(place_of(k))] = value
            pre_copy(place_of(k), pre_send.at[k], core_peer).start()

        @pl.when(jnp.logical_not(inside))
        def _():
            give[...] = value
            give_copy(k).start()

        return carry

    lax.fori_loop(0, 1 + edge, unit_step, 0)

    row_slots = pl.ds(y * line * 2, line * 2)
    row_tokens = pl.ds(pl.multiple_of(y * (tokens // 2), tokens // 2), tokens // 2)
    row_n = nbuf[row_slots].reshape(tokens // 2, TILE)
    gram_n[...] = contract(row_n, row_n, 0, 0)

    def pre_flow(place, act):
        unit = place + 3 * p - 4 * block
        outside = jnp.logical_or(unit < 0, unit > 3)
        source = jnp.where(edge == 1, unit // 2, unit - 2 * (r - 1))
        gate = 2 - r
        incoming = jnp.logical_or(outside, source != c)

        @pl.when(incoming)
        def _():
            act(pre_copy(place, pre_send.at[3], core_peer), False)

        @pl.when(jnp.logical_and(outside, gate == c))
        def _():
            act(pre_copy(place, pre_send.at[3], core_peer), True)

    def pre_in(copy, forward):
        if forward:
            copy.start()
        else:
            copy.wait_recv()

    def pre_done(copy, forward):
        if forward:
            copy.wait_send()

    for place in range(3):
        pre_flow(place, pre_in)

    cross[...] = contract(pre[row_tokens, :], nbuf[row_slots].reshape(tokens // 2, TILE), 0, 0)

    def other_row(i, carry):
        zs, _ = line_source(jnp.maximum(i - 1, 0))
        zs = jnp.where(i == 0, z, zs)
        slot = slot_of(1 - y, zs, 0)
        for cs in range(2):
            n_to_y(slot + cs).wait_recv()
        piece = nbuf[pl.ds(slot, 2)].reshape(2 * tokens_here, TILE)
        gram_n[...] += contract(piece, piece, 0, 0)
        rows = pl.ds(pl.multiple_of(slot * tokens_here, 2 * tokens_here), 2 * tokens_here)
        cross[...] += contract(pre[rows, :], piece, 0, 0)
        return carry

    lax.fori_loop(0, line, other_row, 0)

    scale_n = scaled_factor(gram_n, low_n, tokens)

    def result(h):
        rows = cross[pl.ds(pl.multiple_of(h * strip, strip), strip), :]
        first = contract(rows.astype(jnp.bfloat16), low_n[...], 1, 0)
        second = contract(first.astype(jnp.bfloat16), low_n[...], 1, 0)
        third = contract(second.astype(jnp.bfloat16), low_n[...], 1, 0)
        return scale_n * (4.0 * rows - 6.0 * first + 4.0 * second - third)

    def energy(value):
        total = jnp.sum((value * value).reshape(strip // 8, 8, TILE), axis=0)
        part = total[:, :128]
        for i in range(1, TILE // 128):
            part = part + total[:, i * 128 : (i + 1) * 128]
        return part

    theirs[...] = result(1 - c)
    swap = remote(theirs, arrived, swap_send.at[0], swap_recv.at[0], core_peer)
    swap.start()
    mine[...] = result(c)
    squares[flat] = energy(theirs[...]) + energy(mine[...])

    def sq_copy(d, slot):
        target = (flat + d) % devices
        return remote(
            squares.at[slot],
            squares.at[slot],
            sq_send.at[d],
            sq_recv.at[slot],
            (target // owners, target % owners),
        )

    def sq_start(d, carry):
        sq_copy(d, flat).start()
        return carry

    def sq_wait(d, carry):
        sq_copy(d, (flat + d) % devices).wait_recv()
        return carry

    lax.fori_loop(1, devices, sq_start, 0)
    lax.fori_loop(1, devices, sq_wait, 0)
    total = jnp.sum(squares[...], axis=0)
    total = jnp.sum(jnp.sum(total, axis=0, keepdims=True), axis=1, keepdims=True)
    final = lax.rsqrt(total / (width * out_width) + 1e-06)
    swap.wait_recv()
    update_ref[:, pl.ds(pl.multiple_of(c * TILE, TILE), TILE)] = (mine[...] * final).astype(
        jnp.bfloat16
    )
    update_ref[:, pl.ds(pl.multiple_of((1 - c) * TILE, TILE), TILE)] = (
        arrived[...] * final
    ).astype(jnp.bfloat16)

    def sq_drain(d, carry):
        sq_copy(d, flat).wait_send()
        return carry

    lax.fori_loop(1, devices, sq_drain, 0)
    swap.wait_send()
    n_pass.wait_send()
    own_out(own_slot, drain)
    own_out(core_slot, drain)

    def line_drain(i, carry):
        zs, below = line_source(i)
        for cs in range(2):
            line_out(slot_of(y, zs, cs), below, drain)
        return carry

    lax.fori_loop(0, line - 1, line_drain, 0)
    c_own.wait_send()

    def c_drain(k):
        slot = c_in_slot(k, 0)
        c_out(k).wait_send()
        c_relay(slot, c_x, x_peer).wait_send()
        c_relay(slot, c_core, core_peer).wait_send()

    def c_shared_drain(k):
        c_relay(c_in_slot(k, 1), c_core, core_peer).wait_send()

    for k in range(1, line):
        c_drain(k)
        c_shared_drain(k)

    @pl.when(x == 1)
    def _():
        c_drain(0)

    @pl.when(x == 0)
    def _():
        c_shared_drain(0)

    def unit_drain(k, carry):
        inside = is_mine(k)

        @pl.when(inside)
        def _():
            pre_copy(place_of(k), pre_send.at[k], core_peer).wait_send()

        @pl.when(jnp.logical_not(inside))
        def _():
            give_copy(k).wait_send()

        return carry

    lax.fori_loop(0, 1 + edge, unit_drain, 0)
    for place in range(3):
        pre_flow(place, pre_done)


def whole(groups, owners, hidden, norm_gain, cotangent):
    tokens_here, width = hidden.shape
    out_width = cotangent.shape[1]
    tokens = groups * tokens_here
    strip = out_width // groups
    line = groups // 4
    low, high = jnp.bfloat16, jnp.float32
    dma = pltpu.SemaphoreType.DMA
    return pl.pallas_call(
        functools.partial(whole_kernel, (groups, owners, tokens_here, width, out_width)),
        out_shape=jax.ShapeDtypeStruct((strip, width // owners), low),
        in_specs=[
            pl.BlockSpec(memory_space=pl.ANY),
            pl.BlockSpec(memory_space=pltpu.VMEM),
            pl.BlockSpec(memory_space=pl.ANY),
        ],
        out_specs=pl.BlockSpec(memory_space=pltpu.VMEM),
        scratch_shapes=[
            pltpu.VMEM((tokens_here, width), low),
            pltpu.VMEM((groups, tokens_here, TILE), low),
            pltpu.VMEM((groups, tokens_here, TILE), low),
            pltpu.VMEM((tokens_here, TILE), low),
            pltpu.VMEM((TILE, TILE), high),
            pltpu.VMEM((TILE, TILE), high),
            pltpu.VMEM((TILE, TILE), low),
            pltpu.VMEM((TILE, TILE), low),
            pltpu.VMEM((tokens, 2 * strip), low),
            pltpu.VMEM((tokens, UNIT), low),
            pltpu.VMEM((2 * strip, TILE), high),
            pltpu.VMEM((strip, TILE), high),
            pltpu.VMEM((strip, TILE), high),
            pltpu.VMEM((strip, TILE), high),
            pltpu.VMEM((groups * owners, 8, 128), high),
            dma((2,)),
            dma((line,)),
            dma((groups,)),
            dma((groups,)),
            dma((groups,)),
            dma((1,)),
            dma((groups,)),
            dma((groups,)),
            dma((groups,)),
            dma((groups,)),
            dma((4,)),
            dma((3,)),
            dma((1,)),
            dma((1,)),
            dma((groups * owners,)),
            dma((groups * owners,)),
        ],
        compiler_params=pltpu.CompilerParams(
            collective_id=0, has_side_effects=True, vmem_limit_bytes=60 * 2**20
        ),
    )(hidden, norm_gain.reshape(1, width), cotangent)


def fits(groups, owners, width, out_width):
    line = groups // 4
    return (
        owners == 2
        and width == 2 * owners * TILE
        and groups % 8 == 0
        and line & (line - 1) == 0
        and line >= 4
        and 8 * out_width == 3 * TILE * groups
    )


def step(hidden, norm_gain, cotangent):
    groups, owners = lax.axis_size("dp"), lax.axis_size("owner")
    if fits(groups, owners, hidden.shape[1], cotangent.shape[1]):
        return whole(groups, owners, hidden, norm_gain, cotangent)
    return shards(hidden, norm_gain, cotangent)


def solution(mesh):
    in_specs = (P("dp", None), P(), P("dp", None))
    out_specs = P("dp", "owner")
    return jax.shard_map(step, mesh=mesh, in_specs=in_specs, out_specs=out_specs, check_vma=False)
```

```python
import functools

import jax
import jax.numpy as jnp
from jax import lax
from jax.experimental import pallas as pl
from jax.experimental.pallas import tpu as pltpu
from jax.sharding import PartitionSpec as P

TILE = 1024


DAMPING = 0.1


def contract(left, right, left_dim, right_dim):
    return lax.dot_general(
        left, right, (((left_dim,), (right_dim,)), ((), ())), preferred_element_type=jnp.float32
    )


def inverse_of(piece, tokens):
    identity = jnp.eye(TILE, dtype=jnp.float32)
    matrix = contract(piece, piece, 0, 0) / tokens + DAMPING * identity
    scale = 1.0 / jnp.max(jnp.sum(jnp.abs(matrix), axis=1))
    first = 2.0 * scale * identity - (scale * scale) * matrix
    first_low = first.astype(jnp.bfloat16)
    matrix_low = matrix.astype(jnp.bfloat16)
    product = contract(first_low, matrix_low, 1, 0).astype(jnp.bfloat16)
    return (2.0 * first - contract(product, first_low, 1, 0)).astype(jnp.bfloat16)


def shards(hidden, norm_gain, cotangent):
    owners = lax.axis_size("owner")
    position = lax.axis_index("owner")
    groups = lax.axis_size("dp")
    group = lax.axis_index("dp")
    tokens_here = hidden.shape[0]
    tokens = tokens_here * groups
    width = hidden.shape[1]
    out_width = cotangent.shape[1]
    strip = out_width // groups
    own = width // owners
    in_width = max(own, TILE)

    firsts = jnp.array([(g * strip) // TILE for g in range(groups)], jnp.int32)
    lasts = jnp.array([((g + 1) * strip - 1) // TILE for g in range(groups)], jnp.int32)
    odd = lax.rem(position, 2) == 1
    wanted = jnp.where(odd, lasts, firsts)
    outgoing = jnp.stack(
        [
            lax.dynamic_slice_in_dim(cotangent, wanted[g] * TILE, TILE, 1)
            for g in range(groups)
        ]
    )
    out_piece = lax.all_to_all(outgoing, "dp", 0, 0, tiled=True).reshape(tokens, TILE)

    states = hidden.astype(jnp.float32)
    normed = (
        states * lax.rsqrt(jnp.mean(states * states, axis=1, keepdims=True) + 1e-05) * norm_gain
    ).astype(jnp.bfloat16)
    in_start = (position * own) // TILE * TILE
    mine = lax.dynamic_slice_in_dim(normed, in_start, in_width, 1)
    in_piece = lax.all_gather(mine, "dp", axis=0, tiled=True)

    out_inverse = inverse_of(out_piece, tokens)
    padded = jnp.pad(out_inverse, ((0, 0), (strip, strip)))
    offset = group * strip - wanted[group] * TILE
    strip_inverse = lax.dynamic_slice_in_dim(padded, offset + strip, strip, 1)
    part = contract(out_piece, strip_inverse, 1, 0).astype(jnp.bfloat16)
    other = lax.ppermute(part, "owner", [(o, o ^ 1) for o in range(owners)])
    column_block = (group * strip + jnp.arange(strip, dtype=jnp.int32)) // TILE
    pre_out = jnp.where((column_block == wanted[group])[None, :], part, other)

    results = []
    for block in range(in_width // TILE):
        piece = in_piece[:, block * TILE : (block + 1) * TILE]
        inverse = inverse_of(piece, tokens)
        if own < TILE:
            inverse = lax.dynamic_slice_in_dim(inverse, position * own - in_start, own, 1)
        cross = contract(pre_out, piece, 0, 0).astype(jnp.bfloat16)
        results.append(contract(cross, inverse, 1, 0))
    summed = jnp.concatenate(results, axis=1)
    squares = lax.psum(jnp.sum(summed * summed), ("dp", "owner"))
    return (summed * lax.rsqrt(squares / (width * out_width) + 1e-06)).astype(jnp.bfloat16)


MESH = pl.DeviceIdType.MESH
UNIT = TILE // 4
CHUNK = 128
EARLY = (1, 2, 3)
MIDDLE = (
    ("d0", "d2", "d1", "s2", "L10", "s0", "d3", "L00", "s1", "L11", "L01", "s3",),
    (),
    ("L20", "S0",),
    ("L21",),
    (),
    ("Y", "S1", "P", "S2",),
)
END = (
    ("d1", "S2", "d2", "s1", "d0", "S0", "Y", "s0", "d3", "L00", "s3", "L01", "s2",),
    ("L10",),
    (),
    ("S1", "L20",),
    ("P", "L11", "L21",),
    (),
)


def flipped(value, mask):
    for bit in range(mask.bit_length()):
        if (mask >> bit) & 1:
            value = value + (1 - 2 * ((value // 2**bit) % 2)) * 2**bit
    return value


def matrix_chunk(gram, tokens, i):
    shape = (CHUNK, TILE)
    row = lax.broadcasted_iota(jnp.int32, shape, 0) + i * CHUNK
    column = lax.broadcasted_iota(jnp.int32, shape, 1)
    rows = pl.ds(pl.multiple_of(i * CHUNK, CHUNK), CHUNK)
    return gram[rows, :] * (1.0 / tokens) + jnp.where(row == column, DAMPING, 0.0)


def scaled_factor(gram, low, tokens):
    def add(i, total):
        return total + jnp.sum(jnp.abs(matrix_chunk(gram, tokens, i)), axis=0, keepdims=True)

    sums = lax.fori_loop(0, TILE // CHUNK, add, jnp.zeros((1, TILE), jnp.float32))
    scale = 1.0 / jnp.max(sums, axis=1, keepdims=True)

    def put(i, carry):
        rows = pl.ds(pl.multiple_of(i * CHUNK, CHUNK), CHUNK)
        low[rows, :] = (scale * matrix_chunk(gram, tokens, i)).astype(jnp.bfloat16)
        return carry

    lax.fori_loop(0, TILE // CHUNK, put, 0)
    return scale


def whole_kernel(
    sizes,
    hidden_ref,
    gain_ref,
    cotangent_ref,
    update_ref,
    states,
    cbuf,
    nbuf,
    other_n,
    gram_c,
    gram_n,
    low_c,
    low_n,
    pre,
    give,
    cross,
    second_low,
    mine,
    theirs,
    arrived,
    squares,
    meet,
    load_sem,
    c_send,
    c_x,
    c_core,
    c_recv,
    n_core,
    n_up,
    n_down,
    n_y,
    n_recv,
    pre_send,
    pre_recv,
    swap_send,
    swap_recv,
    sq_send,
    sq_recv,
):
    groups, owners, tokens_here, width, out_width = sizes
    tokens = groups * tokens_here
    line = groups // 4
    strip = out_width // groups
    own = width // owners
    me = lax.axis_index("dp")
    x = lax.axis_index("owner")
    z = me // 4
    y = (me // 2) % 2
    c = me % 2
    devices = groups * owners
    flat = me * owners + x

    def slot_of(y_, z_, c_):
        return (y_ * line + z_) * 2 + c_

    def device(x_, y_, z_, c_):
        return ((z_ * 2 + y_) * 2 + c_, x_)

    def block_of(p):
        return 3 * (p // 4) + (p % 4 + 1) // 2

    def remote(src, dst, send, recv, target):
        return pltpu.make_async_remote_copy(
            src_ref=src,
            dst_ref=dst,
            send_sem=send,
            recv_sem=recv,
            device_id=target,
            device_id_type=MESH,
        )

    own_slot = slot_of(y, z, c)
    core_slot = slot_of(y, z, 1 - c)
    core_peer = device(x, y, z, 1 - c)
    x_peer = device(1 - x, y, z, c)

    load = pltpu.make_async_copy(hidden_ref, states, load_sem.at[0])
    load.start()

    barrier = pltpu.get_barrier_semaphore()

    def greet(target):
        pl.semaphore_signal(barrier, inc=1, device_id=target, device_id_type=MESH)

    greet(core_peer)
    greet(x_peer)
    greet(device(x, 1 - y, z, c))
    for k in range(1, line):
        zd = flipped(z, k)
        greet(device(x, (y + x + z + zd) % 2, zd, c))

    @pl.when(z + 1 < line)
    def _():
        greet(device(x, y, z + 1, c))

    @pl.when(z > 0)
    def _():
        greet(device(x, y, z - 1, c))

    pl.semaphore_wait(barrier, 2 + line + jnp.where(z + 1 < line, 1, 0) + jnp.where(z > 0, 1, 0))

    def block_columns(y_, z_):
        return pl.ds(pl.multiple_of(block_of(z_ * 2 + y_) * TILE, TILE), TILE)

    def c_out(k):
        zd = flipped(z, k)
        yd = (y + x + z + zd) % 2
        return remote(
            cotangent_ref.at[:, block_columns(yd, zd)],
            cbuf.at[own_slot],
            c_send.at[k],
            c_recv.at[own_slot],
            device(x, yd, zd, c),
        )

    def c_in_slot(k, through):
        zs = flipped(z, k)
        ys = (y + x + through + z + zs) % 2
        return slot_of(ys, zs, c)

    def c_relay(slot, sems, target):
        return remote(cbuf.at[slot], cbuf.at[slot], sems.at[slot], c_recv.at[slot], target)

    early = EARLY
    for k in early:
        c_out(k).start()

    @pl.when(x == 1)
    def _():
        c_out(0).start()

    local = pltpu.make_async_copy(
        cotangent_ref.at[:, block_columns(y, z)], cbuf.at[own_slot], load_sem.at[1]
    )
    local.start()
    c_own = remote(
        cotangent_ref.at[:, block_columns(y, z)],
        cbuf.at[own_slot],
        c_core.at[own_slot],
        c_recv.at[own_slot],
        core_peer,
    )
    c_own.start()

    load.wait()
    part = 16
    kept = pl.ds(pl.multiple_of(x * own + c * TILE, TILE), TILE)
    passed = pl.ds(pl.multiple_of(x * own + (1 - c) * TILE, TILE), TILE)

    def normalize(i, carry):
        rows = pl.ds(pl.multiple_of(i * part, part), part)
        full = states[rows, :].astype(jnp.float32)
        factor = lax.rsqrt(jnp.sum(full * full, axis=1, keepdims=True) * (1.0 / width) + 1e-05)
        for columns, put in ((passed, other_n), (kept, nbuf.at[own_slot])):
            piece = states[rows, columns].astype(jnp.float32) * factor * gain_ref[:, columns]
            put[rows, :] = piece.astype(jnp.bfloat16)
        return carry

    lax.fori_loop(0, tokens_here // part, normalize, 0)
    n_pass = remote(other_n, nbuf.at[own_slot], n_core.at[0], n_recv.at[own_slot], core_peer)
    n_pass.start()

    def n_copy(slot, sems, target):
        return remote(nbuf.at[slot], nbuf.at[slot], sems.at[slot], n_recv.at[slot], target)

    def n_to_y(slot):
        return n_copy(slot, n_y, device(x, 1 - y, z, c))

    def n_to_up(slot):
        return n_copy(slot, n_up, device(x, y, z + 1, c))

    def n_to_down(slot):
        return n_copy(slot, n_down, device(x, y, z - 1, c))

    def own_out(slot, act):
        act(n_to_y(slot))

        @pl.when(z + 1 < line)
        def _():
            act(n_to_up(slot))

        @pl.when(z > 0)
        def _():
            act(n_to_down(slot))

    def start(copy):
        copy.start()

    def drain(copy):
        copy.wait_send()

    own_out(own_slot, start)
    n_to_y(core_slot).wait_recv()
    own_out(core_slot, start)
    for k in range(1, line):
        if k not in early:
            c_out(k).start()

    def line_source(i):
        low = jnp.minimum(z, line - 1 - z)
        near = i < 2 * low
        distance = jnp.where(near, i // 2 + 1, i + 1 - low)
        below = jnp.where(near, i % 2 == 0, z > low)
        return jnp.where(below, z - distance, z + distance), below

    def line_out(slot, below, act):
        @pl.when(jnp.logical_and(below, z + 1 < line))
        def _():
            act(n_to_up(slot))

        @pl.when(jnp.logical_and(jnp.logical_not(below), z > 0))
        def _():
            act(n_to_down(slot))

    is_end = jnp.logical_or(z == 0, z == line - 1)

    def from_end(zs):
        return jnp.logical_or(zs == 0, zs == line - 1)

    def line_piece(i, cs, act, wait):
        zs, below = line_source(i)
        slot = slot_of(y, zs, cs)
        if wait:
            n_to_y(slot).wait_recv()
        line_out(slot, below, act)
        if cs == 0:

            @pl.when(jnp.logical_not(from_end(zs)))
            def _():
                act(n_to_y(slot))
        else:
            act(n_to_y(slot))

    def crossed_piece(i, act, wait):
        zs, below = line_source(i)

        @pl.when(jnp.logical_and(from_end(zs), jnp.logical_not(is_end)))
        def _():
            slot = slot_of(1 - y, zs, 0)
            if wait:
                n_to_y(slot).wait_recv()
            line_out(slot, below, act)

    def crossed_here(act, wait):
        @pl.when(is_end)
        def _():
            slot = slot_of(1 - y, z, 0)
            if wait:
                n_to_y(slot).wait_recv()
            line_out(slot, z == 0, act)

    def c_direct(k):
        slot = c_in_slot(k, 0)
        c_relay(slot, c_x, x_peer).wait_recv()
        c_relay(slot, c_x, x_peer).start()
        c_relay(slot, c_core, core_peer).start()

    def c_from_core(i, carry):
        slot = 2 * i + 1 - c
        c_relay(slot, c_core, core_peer).wait_recv()
        return carry

    def direct_zero():
        @pl.when(x == 1)
        def _():
            c_direct(0)

    def c_shared(k):
        slot = c_in_slot(k, 1)
        c_relay(slot, c_core, core_peer).wait_recv()
        c_relay(slot, c_core, core_peer).start()

    def shared_zero():
        @pl.when(x == 0)
        def _():
            c_shared(0)

    def gram_rows(i):
        block_tokens = cbuf[...].reshape(tokens, TILE)
        part = slice(i * TILE // 2, (i + 1) * TILE // 2)
        gram_c[part, :] = contract(block_tokens[:, part], block_tokens, 0, 0)

    p = z * 2 + y
    r = p % 4
    edge = jnp.where(jnp.logical_or(r == 0, r == 3), 1, 0)
    block = block_of(p)

    def unit_of(k):
        return edge * (3 * c + k * (1 - 2 * c)) + (1 - edge) * (2 * (r - 1) + c)

    def place_of(k):
        return 4 * block + unit_of(k) - 3 * p

    def strip_columns(place):
        return pl.ds(pl.multiple_of(place * UNIT, UNIT), UNIT)

    def pre_copy(place, send, target):
        view = pre.at[:, strip_columns(place)]
        return remote(view, view, send, pre_recv.at[place], target)

    half = tokens // 2

    def half_rows(h):
        return pl.ds(pl.multiple_of(h * half, half), half)

    def give_copy():
        place = place_of(0) - 3 * (1 - 2 * y)
        return remote(
            give,
            pre.at[half_rows(x), strip_columns(place)],
            pre_send.at[2],
            pre_recv.at[3 + x],
            device(x, 1 - y, z, c),
        )

    outer_place = (r - 1) * 2

    def outer_copy(h, send, target):
        view = pre.at[half_rows(h), strip_columns(outer_place)]
        return remote(view, view, pre_send.at[send], pre_recv.at[3 + h], target)

    def outer_first():
        @pl.when(jnp.logical_and(edge == 0, c == 2 - r))
        def _():
            outer_copy(x, 3, x_peer).wait_recv()
            outer_copy(x, 3, x_peer).start()
            outer_copy(x, 4, core_peer).start()

    def outer_rest():
        @pl.when(jnp.logical_and(edge == 0, c == 2 - r))
        def _():
            outer_copy(1 - x, 5, core_peer).wait_recv()
            outer_copy(1 - x, 5, core_peer).start()

        @pl.when(jnp.logical_and(edge == 0, c == r - 1))
        def _():
            outer_copy(0, 3, core_peer).wait_recv()
            outer_copy(1, 3, core_peer).wait_recv()

    def outer_drain():
        @pl.when(jnp.logical_and(edge == 0, c == 2 - r))
        def _():
            outer_copy(x, 3, x_peer).wait_send()
            outer_copy(x, 4, core_peer).wait_send()
            outer_copy(1 - x, 5, core_peer).wait_send()

    def unit_inverse(k, scale_c):
        unit = unit_of(k)
        first = low_c[:, pl.ds(pl.multiple_of(unit * UNIT, UNIT), UNIT)]
        second = contract(low_c[...], first, 1, 0)
        third = contract(low_c[...], second.astype(jnp.bfloat16), 1, 0)
        row = lax.broadcasted_iota(jnp.int32, (TILE, UNIT), 0)
        column = lax.broadcasted_iota(jnp.int32, (TILE, UNIT), 1) + unit * UNIT
        start4 = jnp.where(row == column, 4.0, 0.0)
        inverse = scale_c * (start4 - 6.0 * first.astype(jnp.float32) + 4.0 * second - third)
        return inverse.astype(jnp.bfloat16)

    def is_mine(k):
        place = place_of(k)
        return jnp.logical_and(place >= 0, place < 3)

    def unit_step(k, scale_c):
        inverse = unit_inverse(k, scale_c)
        inside = is_mine(k)

        @pl.when(inside)
        def _():
            whole = cbuf[...].reshape(tokens, TILE)
            pre[:, strip_columns(place_of(k))] = contract(whole, inverse, 1, 0).astype(jnp.bfloat16)
            pre_copy(place_of(k), pre_send.at[k], core_peer).start()

        @pl.when(jnp.logical_not(inside))
        def _():
            rows = cbuf[pl.ds(x * (groups // 2), groups // 2)].reshape(half, TILE)
            give[...] = contract(rows, inverse, 1, 0).astype(jnp.bfloat16)
            give_copy().start()

    row_slots = pl.ds(y * line * 2, line * 2)
    row_tokens = pl.ds(pl.multiple_of(y * (tokens // 2), tokens // 2), tokens // 2)

    def move(token):
        kind = token[0]
        if kind == "d":
            k = int(token[1])
            if k:
                c_direct(k)
            else:
                direct_zero()
        elif kind == "s":
            k = int(token[1])
            if k:
                c_shared(k)
            else:
                shared_zero()
        elif kind == "L":
            line_piece(int(token[1]), int(token[2]), start, True)
        elif kind == "S":
            crossed_piece(int(token[1]), start, True)
        elif kind == "Y":
            crossed_here(start, True)
        elif kind == "P":
            outer_first()

    def moves(stage):
        @pl.when(is_end)
        def _():
            for token in END[stage]:
                move(token)

        @pl.when(jnp.logical_not(is_end))
        def _():
            for token in MIDDLE[stage]:
                move(token)

    moves(0)
    lax.fori_loop(0, groups // 2, c_from_core, 0)
    local.wait()
    gram_rows(0)
    moves(1)
    gram_rows(1)
    scale_c = scaled_factor(gram_c, low_c, tokens)
    moves(2)
    unit_step(0, scale_c)
    moves(3)

    @pl.when(edge == 1)
    def _():
        unit_step(1, scale_c)

    moves(4)

    def more(i, carry):
        for cs in range(2):
            line_piece(i, cs, start, True)
        crossed_piece(i, start, True)
        return carry

    lax.fori_loop(3, line - 1, more, 0)
    row_n = nbuf[row_slots].reshape(tokens // 2, TILE)
    gram_n[...] = contract(row_n, row_n, 0, 0)
    moves(5)

    def pre_in(place):
        unit = place + 3 * p - 4 * block
        inside = jnp.logical_and(unit >= 0, unit <= 3)
        source = jnp.where(edge == 1, unit // 2, unit - 2 * (r - 1))

        @pl.when(jnp.logical_and(inside, source != c))
        def _():
            pre_copy(place, pre_send.at[0], core_peer).wait_recv()

    for place in range(3):
        pre_in(place)
    outer_rest()

    cross[...] = contract(pre[row_tokens, :], nbuf[row_slots].reshape(tokens // 2, TILE), 0, 0)

    def other_row(i, carry):
        zs, _ = line_source(jnp.maximum(i - 1, 0))
        zs = jnp.where(i == 0, z, zs)
        slot = slot_of(1 - y, zs, 0)

        seen = jnp.where(i == 0, is_end, jnp.logical_and(from_end(zs), jnp.logical_not(is_end)))

        @pl.when(jnp.logical_not(seen))
        def _():
            n_to_y(slot).wait_recv()

        n_to_y(slot + 1).wait_recv()
        piece = nbuf[pl.ds(slot, 2)].reshape(2 * tokens_here, TILE)
        gram_n[...] += contract(piece, piece, 0, 0)
        rows = pl.ds(pl.multiple_of(slot * tokens_here, 2 * tokens_here), 2 * tokens_here)
        cross[...] += contract(pre[rows, :], piece, 0, 0)
        return carry

    lax.fori_loop(0, line, other_row, 0)

    pl.semaphore_signal(meet, inc=1, device_id=x_peer, device_id_type=MESH)
    scale_n = scaled_factor(gram_n, low_n, tokens)

    first = contract(cross[...].astype(jnp.bfloat16), low_n[...], 1, 0)
    cross[...] = 4.0 * cross[...] - 6.0 * first
    second = contract(first.astype(jnp.bfloat16), low_n[...], 1, 0)
    cross[...] += 4.0 * second
    second_low[...] = second.astype(jnp.bfloat16)

    def result(h):
        rows = pl.ds(pl.multiple_of(h * strip, strip), strip)
        third = contract(second_low[rows, :], low_n[...], 1, 0)
        return scale_n * (cross[rows, :] - third)

    def energy(value):
        total = jnp.sum((value * value).reshape(strip // 8, 8, TILE), axis=0)
        part = total[:, :128]
        for i in range(1, TILE // 128):
            part = part + total[:, i * 128 : (i + 1) * 128]
        return part

    theirs[...] = result(1 - c)
    swap = remote(theirs, arrived, swap_send.at[0], swap_recv.at[0], core_peer)
    swap.start()
    mine[...] = result(c)
    squares[flat] = energy(theirs[...]) + energy(mine[...])

    def sq_copy(d, slot):
        target = (flat + d) % devices
        return remote(
            squares.at[slot],
            squares.at[slot],
            sq_send.at[d],
            sq_recv.at[slot],
            (target // owners, target % owners),
        )

    def sq_start(d, carry):
        sq_copy(d, flat).start()
        return carry

    def sq_wait(d, carry):
        sq_copy(d, (flat + d) % devices).wait_recv()
        return carry

    pl.semaphore_wait(meet, 1)
    lax.fori_loop(1, devices, sq_start, 0)
    lax.fori_loop(1, devices, sq_wait, 0)
    total = jnp.sum(squares[...], axis=0)
    total = jnp.sum(jnp.sum(total, axis=0, keepdims=True), axis=1, keepdims=True)
    final = lax.rsqrt(total / (width * out_width) + 1e-06)
    update_ref[:, pl.ds(pl.multiple_of(c * TILE, TILE), TILE)] = (mine[...] * final).astype(
        jnp.bfloat16
    )
    swap.wait_recv()
    update_ref[:, pl.ds(pl.multiple_of((1 - c) * TILE, TILE), TILE)] = (
        arrived[...] * final
    ).astype(jnp.bfloat16)

    def sq_drain(d, carry):
        sq_copy(d, flat).wait_send()
        return carry

    lax.fori_loop(1, devices, sq_drain, 0)
    swap.wait_send()
    n_pass.wait_send()
    own_out(own_slot, drain)
    own_out(core_slot, drain)

    def line_drain(i, carry):
        for cs in range(2):
            line_piece(i, cs, drain, False)
        crossed_piece(i, drain, False)
        return carry

    lax.fori_loop(0, line - 1, line_drain, 0)
    crossed_here(drain, False)
    c_own.wait_send()

    def c_drain(k):
        slot = c_in_slot(k, 0)
        c_out(k).wait_send()
        c_relay(slot, c_x, x_peer).wait_send()
        c_relay(slot, c_core, core_peer).wait_send()

    def c_shared_drain(k):
        c_relay(c_in_slot(k, 1), c_core, core_peer).wait_send()

    for k in range(1, line):
        c_drain(k)
        c_shared_drain(k)

    @pl.when(x == 1)
    def _():
        c_drain(0)

    @pl.when(x == 0)
    def _():
        c_shared_drain(0)

    def unit_drain(k, carry):
        inside = is_mine(k)

        @pl.when(inside)
        def _():
            pre_copy(place_of(k), pre_send.at[k], core_peer).wait_send()

        @pl.when(jnp.logical_not(inside))
        def _():
            give_copy().wait_send()

        return carry

    lax.fori_loop(0, 1 + edge, unit_drain, 0)
    outer_drain()


def whole(groups, owners, hidden, norm_gain, cotangent):
    tokens_here, width = hidden.shape
    out_width = cotangent.shape[1]
    tokens = groups * tokens_here
    strip = out_width // groups
    line = groups // 4
    low, high = jnp.bfloat16, jnp.float32
    dma = pltpu.SemaphoreType.DMA
    return pl.pallas_call(
        functools.partial(whole_kernel, (groups, owners, tokens_here, width, out_width)),
        out_shape=jax.ShapeDtypeStruct((strip, width // owners), low),
        in_specs=[
            pl.BlockSpec(memory_space=pl.ANY),
            pl.BlockSpec(memory_space=pltpu.VMEM),
            pl.BlockSpec(memory_space=pl.ANY),
        ],
        out_specs=pl.BlockSpec(memory_space=pltpu.VMEM),
        scratch_shapes=[
            pltpu.VMEM((tokens_here, width), low),
            pltpu.VMEM((groups, tokens_here, TILE), low),
            pltpu.VMEM((groups, tokens_here, TILE), low),
            pltpu.VMEM((tokens_here, TILE), low),
            pltpu.VMEM((TILE, TILE), high),
            pltpu.VMEM((TILE, TILE), high),
            pltpu.VMEM((TILE, TILE), low),
            pltpu.VMEM((TILE, TILE), low),
            pltpu.VMEM((tokens, 2 * strip), low),
            pltpu.VMEM((tokens // 2, UNIT), low),
            pltpu.VMEM((2 * strip, TILE), high),
            pltpu.VMEM((2 * strip, TILE), low),
            pltpu.VMEM((strip, TILE), high),
            pltpu.VMEM((strip, TILE), high),
            pltpu.VMEM((strip, TILE), high),
            pltpu.VMEM((groups * owners, 8, 128), high),
            pltpu.SemaphoreType.REGULAR,
            dma((2,)),
            dma((line,)),
            dma((groups,)),
            dma((groups,)),
            dma((groups,)),
            dma((1,)),
            dma((groups,)),
            dma((groups,)),
            dma((groups,)),
            dma((groups,)),
            dma((6,)),
            dma((5,)),
            dma((1,)),
            dma((1,)),
            dma((groups * owners,)),
            dma((groups * owners,)),
        ],
        compiler_params=pltpu.CompilerParams(
            collective_id=0, has_side_effects=True, vmem_limit_bytes=60 * 2**20
        ),
    )(hidden, norm_gain.reshape(1, width), cotangent)


def fits(groups, owners, width, out_width):
    line = groups // 4
    return (
        owners == 2
        and width == 2 * owners * TILE
        and groups % 8 == 0
        and line & (line - 1) == 0
        and line >= 4
        and 8 * out_width == 3 * TILE * groups
    )


def step(hidden, norm_gain, cotangent):
    groups, owners = lax.axis_size("dp"), lax.axis_size("owner")
    if fits(groups, owners, hidden.shape[1], cotangent.shape[1]):
        return whole(groups, owners, hidden, norm_gain, cotangent)
    return shards(hidden, norm_gain, cotangent)


def solution(mesh):
    in_specs = (P("dp", None), P(), P("dp", None))
    out_specs = P("dp", "owner")
    return jax.shard_map(step, mesh=mesh, in_specs=in_specs, out_specs=out_specs, check_vma=False)
```

```python
import functools

import jax
import jax.numpy as jnp
from jax import lax
from jax.experimental import pallas as pl
from jax.experimental.pallas import tpu as pltpu
from jax.sharding import PartitionSpec as P

TILE = 1024


DAMPING = 0.1


def contract(left, right, left_dim, right_dim):
    return lax.dot_general(
        left, right, (((left_dim,), (right_dim,)), ((), ())), preferred_element_type=jnp.float32
    )


def inverse_of(piece, tokens):
    identity = jnp.eye(TILE, dtype=jnp.float32)
    matrix = contract(piece, piece, 0, 0) / tokens + DAMPING * identity
    scale = 1.0 / jnp.max(jnp.sum(jnp.abs(matrix), axis=1))
    first = 2.0 * scale * identity - (scale * scale) * matrix
    first_low = first.astype(jnp.bfloat16)
    matrix_low = matrix.astype(jnp.bfloat16)
    product = contract(first_low, matrix_low, 1, 0).astype(jnp.bfloat16)
    return (2.0 * first - contract(product, first_low, 1, 0)).astype(jnp.bfloat16)


def shards(hidden, norm_gain, cotangent):
    owners = lax.axis_size("owner")
    position = lax.axis_index("owner")
    groups = lax.axis_size("dp")
    group = lax.axis_index("dp")
    tokens_here = hidden.shape[0]
    tokens = tokens_here * groups
    width = hidden.shape[1]
    out_width = cotangent.shape[1]
    strip = out_width // groups
    own = width // owners
    in_width = max(own, TILE)

    firsts = jnp.array([(g * strip) // TILE for g in range(groups)], jnp.int32)
    lasts = jnp.array([((g + 1) * strip - 1) // TILE for g in range(groups)], jnp.int32)
    odd = lax.rem(position, 2) == 1
    wanted = jnp.where(odd, lasts, firsts)
    outgoing = jnp.stack(
        [
            lax.dynamic_slice_in_dim(cotangent, wanted[g] * TILE, TILE, 1)
            for g in range(groups)
        ]
    )
    out_piece = lax.all_to_all(outgoing, "dp", 0, 0, tiled=True).reshape(tokens, TILE)

    states = hidden.astype(jnp.float32)
    normed = (
        states * lax.rsqrt(jnp.mean(states * states, axis=1, keepdims=True) + 1e-05) * norm_gain
    ).astype(jnp.bfloat16)
    in_start = (position * own) // TILE * TILE
    mine = lax.dynamic_slice_in_dim(normed, in_start, in_width, 1)
    in_piece = lax.all_gather(mine, "dp", axis=0, tiled=True)

    out_inverse = inverse_of(out_piece, tokens)
    padded = jnp.pad(out_inverse, ((0, 0), (strip, strip)))
    offset = group * strip - wanted[group] * TILE
    strip_inverse = lax.dynamic_slice_in_dim(padded, offset + strip, strip, 1)
    part = contract(out_piece, strip_inverse, 1, 0).astype(jnp.bfloat16)
    other = lax.ppermute(part, "owner", [(o, o ^ 1) for o in range(owners)])
    column_block = (group * strip + jnp.arange(strip, dtype=jnp.int32)) // TILE
    pre_out = jnp.where((column_block == wanted[group])[None, :], part, other)

    results = []
    for block in range(in_width // TILE):
        piece = in_piece[:, block * TILE : (block + 1) * TILE]
        inverse = inverse_of(piece, tokens)
        if own < TILE:
            inverse = lax.dynamic_slice_in_dim(inverse, position * own - in_start, own, 1)
        cross = contract(pre_out, piece, 0, 0).astype(jnp.bfloat16)
        results.append(contract(cross, inverse, 1, 0))
    summed = jnp.concatenate(results, axis=1)
    squares = lax.psum(jnp.sum(summed * summed), ("dp", "owner"))
    return (summed * lax.rsqrt(squares / (width * out_width) + 1e-06)).astype(jnp.bfloat16)


MESH = pl.DeviceIdType.MESH
UNIT = TILE // 4
CHUNK = 128
EARLY = (1, 2, 3)
MIDDLE = (
    ("d0", "d2", "d1", "s2", "L10", "s0", "d3", "L00", "s1", "L11", "L01", "s3",),
    (),
    ("L20", "S0",),
    ("L21",),
    (),
    ("Y", "S1", "P", "S2",),
)
END = (
    ("d1", "S2", "d2", "s1", "d0", "S0", "Y", "s0", "d3", "L00", "s3", "L01", "s2",),
    ("L10",),
    (),
    ("S1", "L20",),
    ("P", "L11", "L21",),
    (),
)


def flipped(value, mask):
    for bit in range(mask.bit_length()):
        if (mask >> bit) & 1:
            value = value + (1 - 2 * ((value // 2**bit) % 2)) * 2**bit
    return value


def rounded_factor(gram, low, tokens):
    row = lax.broadcasted_iota(jnp.int32, (CHUNK, CHUNK), 0)
    column = lax.broadcasted_iota(jnp.int32, (CHUNK, CHUNK), 1)
    damping = jnp.where(row == column, DAMPING, 0.0)

    def put(i, total):
        rows = pl.ds(pl.multiple_of(i * CHUNK, CHUNK), CHUNK)
        matrix = gram[rows, :] * (1.0 / tokens)
        low[rows, :] = matrix.astype(jnp.bfloat16)
        low[rows, rows] = (gram[rows, rows] * (1.0 / tokens) + damping).astype(jnp.bfloat16)
        folded = jnp.sum(jnp.abs(matrix).reshape(CHUNK // 8, 8, TILE), axis=0)
        return total + folded

    sums = lax.fori_loop(0, TILE // CHUNK, put, jnp.zeros((8, TILE), jnp.float32))
    sums = jnp.sum(sums, axis=0, keepdims=True)
    return 1.0 / (jnp.max(sums, axis=1, keepdims=True) + DAMPING)


def whole_kernel(
    sizes,
    hidden_ref,
    gain_ref,
    cotangent_ref,
    update_ref,
    states,
    cbuf,
    nbuf,
    other_n,
    gram_c,
    gram_n,
    low_c,
    low_n,
    pre,
    give,
    cross,
    second_low,
    mine,
    theirs,
    arrived,
    squares,
    meet,
    load_sem,
    c_send,
    c_x,
    c_core,
    c_recv,
    n_core,
    n_up,
    n_down,
    n_y,
    n_recv,
    pre_send,
    pre_recv,
    swap_send,
    swap_recv,
    sq_send,
    sq_recv,
):
    groups, owners, tokens_here, width, out_width = sizes
    tokens = groups * tokens_here
    line = groups // 4
    strip = out_width // groups
    own = width // owners
    me = lax.axis_index("dp")
    x = lax.axis_index("owner")
    z = me // 4
    y = (me // 2) % 2
    c = me % 2
    devices = groups * owners
    flat = me * owners + x

    def slot_of(y_, z_, c_):
        return (y_ * line + z_) * 2 + c_

    def device(x_, y_, z_, c_):
        return ((z_ * 2 + y_) * 2 + c_, x_)

    def block_of(p):
        return 3 * (p // 4) + (p % 4 + 1) // 2

    def remote(src, dst, send, recv, target):
        return pltpu.make_async_remote_copy(
            src_ref=src,
            dst_ref=dst,
            send_sem=send,
            recv_sem=recv,
            device_id=target,
            device_id_type=MESH,
        )

    own_slot = slot_of(y, z, c)
    core_slot = slot_of(y, z, 1 - c)
    core_peer = device(x, y, z, 1 - c)
    x_peer = device(1 - x, y, z, c)

    load = pltpu.make_async_copy(hidden_ref, states, load_sem.at[0])
    load.start()

    barrier = pltpu.get_barrier_semaphore()

    def greet(target):
        pl.semaphore_signal(barrier, inc=1, device_id=target, device_id_type=MESH)

    greet(core_peer)
    greet(x_peer)
    greet(device(x, 1 - y, z, c))
    for k in range(1, line):
        zd = flipped(z, k)
        greet(device(x, (y + x + z + zd) % 2, zd, c))

    @pl.when(z + 1 < line)
    def _():
        greet(device(x, y, z + 1, c))

    @pl.when(z > 0)
    def _():
        greet(device(x, y, z - 1, c))

    pl.semaphore_wait(barrier, 2 + line + jnp.where(z + 1 < line, 1, 0) + jnp.where(z > 0, 1, 0))

    def block_columns(y_, z_):
        return pl.ds(pl.multiple_of(block_of(z_ * 2 + y_) * TILE, TILE), TILE)

    def c_out(k):
        zd = flipped(z, k)
        yd = (y + x + z + zd) % 2
        return remote(
            cotangent_ref.at[:, block_columns(yd, zd)],
            cbuf.at[own_slot],
            c_send.at[k],
            c_recv.at[own_slot],
            device(x, yd, zd, c),
        )

    def c_in_slot(k, through):
        zs = flipped(z, k)
        ys = (y + x + through + z + zs) % 2
        return slot_of(ys, zs, c)

    def c_relay(slot, sems, target):
        return remote(cbuf.at[slot], cbuf.at[slot], sems.at[slot], c_recv.at[slot], target)

    early = EARLY
    for k in early:
        c_out(k).start()

    @pl.when(x == 1)
    def _():
        c_out(0).start()

    local = pltpu.make_async_copy(
        cotangent_ref.at[:, block_columns(y, z)], cbuf.at[own_slot], load_sem.at[1]
    )
    local.start()
    c_own = remote(
        cotangent_ref.at[:, block_columns(y, z)],
        cbuf.at[own_slot],
        c_core.at[own_slot],
        c_recv.at[own_slot],
        core_peer,
    )
    c_own.start()

    load.wait()
    part = 16
    kept = pl.ds(pl.multiple_of(x * own + c * TILE, TILE), TILE)
    passed = pl.ds(pl.multiple_of(x * own + (1 - c) * TILE, TILE), TILE)

    def normalize(i, carry):
        rows = pl.ds(pl.multiple_of(i * part, part), part)
        full = states[rows, :].astype(jnp.float32)
        factor = lax.rsqrt(jnp.sum(full * full, axis=1, keepdims=True) * (1.0 / width) + 1e-05)
        for columns, put in ((passed, other_n), (kept, nbuf.at[own_slot])):
            piece = states[rows, columns].astype(jnp.float32) * factor * gain_ref[:, columns]
            put[rows, :] = piece.astype(jnp.bfloat16)
        return carry

    lax.fori_loop(0, tokens_here // part, normalize, 0)
    n_pass = remote(other_n, nbuf.at[own_slot], n_core.at[0], n_recv.at[own_slot], core_peer)
    n_pass.start()

    def n_copy(slot, sems, target):
        return remote(nbuf.at[slot], nbuf.at[slot], sems.at[slot], n_recv.at[slot], target)

    def n_to_y(slot):
        return n_copy(slot, n_y, device(x, 1 - y, z, c))

    def n_to_up(slot):
        return n_copy(slot, n_up, device(x, y, z + 1, c))

    def n_to_down(slot):
        return n_copy(slot, n_down, device(x, y, z - 1, c))

    def own_out(slot, act):
        act(n_to_y(slot))

        @pl.when(z + 1 < line)
        def _():
            act(n_to_up(slot))

        @pl.when(z > 0)
        def _():
            act(n_to_down(slot))

    def start(copy):
        copy.start()

    def drain(copy):
        copy.wait_send()

    own_out(own_slot, start)
    n_to_y(core_slot).wait_recv()
    own_out(core_slot, start)
    for k in range(1, line):
        if k not in early:
            c_out(k).start()

    def line_source(i):
        low = jnp.minimum(z, line - 1 - z)
        near = i < 2 * low
        distance = jnp.where(near, i // 2 + 1, i + 1 - low)
        below = jnp.where(near, i % 2 == 0, z > low)
        return jnp.where(below, z - distance, z + distance), below

    def line_out(slot, below, act):
        @pl.when(jnp.logical_and(below, z + 1 < line))
        def _():
            act(n_to_up(slot))

        @pl.when(jnp.logical_and(jnp.logical_not(below), z > 0))
        def _():
            act(n_to_down(slot))

    is_end = jnp.logical_or(z == 0, z == line - 1)

    def from_end(zs):
        return jnp.logical_or(zs == 0, zs == line - 1)

    def line_piece(i, cs, act, wait):
        zs, below = line_source(i)
        slot = slot_of(y, zs, cs)
        if wait:
            n_to_y(slot).wait_recv()
        line_out(slot, below, act)
        if cs == 0:

            @pl.when(jnp.logical_not(from_end(zs)))
            def _():
                act(n_to_y(slot))
        else:
            act(n_to_y(slot))

    def crossed_piece(i, act, wait):
        zs, below = line_source(i)

        @pl.when(jnp.logical_and(from_end(zs), jnp.logical_not(is_end)))
        def _():
            slot = slot_of(1 - y, zs, 0)
            if wait:
                n_to_y(slot).wait_recv()
            line_out(slot, below, act)

    def crossed_here(act, wait):
        @pl.when(is_end)
        def _():
            slot = slot_of(1 - y, z, 0)
            if wait:
                n_to_y(slot).wait_recv()
            line_out(slot, z == 0, act)

    def c_direct(k):
        slot = c_in_slot(k, 0)
        c_relay(slot, c_x, x_peer).wait_recv()
        c_relay(slot, c_x, x_peer).start()
        c_relay(slot, c_core, core_peer).start()

    def c_from_core(i, carry):
        slot = 2 * i + 1 - c
        c_relay(slot, c_core, core_peer).wait_recv()
        return carry

    def direct_zero():
        @pl.when(x == 1)
        def _():
            c_direct(0)

    def c_shared(k):
        slot = c_in_slot(k, 1)
        c_relay(slot, c_core, core_peer).wait_recv()
        c_relay(slot, c_core, core_peer).start()

    def shared_zero():
        @pl.when(x == 0)
        def _():
            c_shared(0)

    def gram_rows(i):
        block_tokens = cbuf[...].reshape(tokens, TILE)
        part = slice(i * TILE // 2, (i + 1) * TILE // 2)
        gram_c[part, :] = contract(block_tokens[:, part], block_tokens, 0, 0)

    p = z * 2 + y
    r = p % 4
    edge = jnp.where(jnp.logical_or(r == 0, r == 3), 1, 0)
    block = block_of(p)

    def unit_of(k):
        return edge * (3 * c + k * (1 - 2 * c)) + (1 - edge) * (2 * (r - 1) + c)

    def place_of(k):
        return 4 * block + unit_of(k) - 3 * p

    def strip_columns(place):
        return pl.ds(pl.multiple_of(place * UNIT, UNIT), UNIT)

    def pre_copy(place, send, target):
        view = pre.at[:, strip_columns(place)]
        return remote(view, view, send, pre_recv.at[place], target)

    half = tokens // 2

    def half_rows(h):
        return pl.ds(pl.multiple_of(h * half, half), half)

    def give_copy():
        place = place_of(0) - 3 * (1 - 2 * y)
        return remote(
            give,
            pre.at[half_rows(x), strip_columns(place)],
            pre_send.at[2],
            pre_recv.at[3 + x],
            device(x, 1 - y, z, c),
        )

    outer_place = (r - 1) * 2

    def outer_copy(h, send, target):
        view = pre.at[half_rows(h), strip_columns(outer_place)]
        return remote(view, view, pre_send.at[send], pre_recv.at[3 + h], target)

    def outer_first():
        @pl.when(jnp.logical_and(edge == 0, c == 2 - r))
        def _():
            outer_copy(x, 3, x_peer).wait_recv()
            outer_copy(x, 3, x_peer).start()
            outer_copy(x, 4, core_peer).start()

    def outer_rest():
        @pl.when(jnp.logical_and(edge == 0, c == 2 - r))
        def _():
            outer_copy(1 - x, 5, core_peer).wait_recv()
            outer_copy(1 - x, 5, core_peer).start()

        @pl.when(jnp.logical_and(edge == 0, c == r - 1))
        def _():
            outer_copy(0, 3, core_peer).wait_recv()
            outer_copy(1, 3, core_peer).wait_recv()

    def outer_drain():
        @pl.when(jnp.logical_and(edge == 0, c == 2 - r))
        def _():
            outer_copy(x, 3, x_peer).wait_send()
            outer_copy(x, 4, core_peer).wait_send()
            outer_copy(1 - x, 5, core_peer).wait_send()

    def unit_inverse(k, scale_c):
        unit = unit_of(k)
        first = low_c[:, pl.ds(pl.multiple_of(unit * UNIT, UNIT), UNIT)]
        second = contract(low_c[...], first, 1, 0)
        third = contract(low_c[...], second.astype(jnp.bfloat16), 1, 0)
        row = lax.broadcasted_iota(jnp.int32, (TILE, UNIT), 0)
        column = lax.broadcasted_iota(jnp.int32, (TILE, UNIT), 1) + unit * UNIT
        start4 = jnp.where(row == column, 4.0, 0.0)
        powers = [scale_c, scale_c**2, scale_c**3, scale_c**4]
        inverse = powers[0] * start4 - (6.0 * powers[1]) * first.astype(jnp.float32)
        inverse = inverse + (4.0 * powers[2]) * second - powers[3] * third
        return inverse.astype(jnp.bfloat16)

    def is_mine(k):
        place = place_of(k)
        return jnp.logical_and(place >= 0, place < 3)

    def unit_step(k, scale_c):
        inverse = unit_inverse(k, scale_c)
        inside = is_mine(k)

        @pl.when(inside)
        def _():
            whole = cbuf[...].reshape(tokens, TILE)
            pre[:, strip_columns(place_of(k))] = contract(whole, inverse, 1, 0).astype(jnp.bfloat16)
            pre_copy(place_of(k), pre_send.at[k], core_peer).start()

        @pl.when(jnp.logical_not(inside))
        def _():
            rows = cbuf[pl.ds(x * (groups // 2), groups // 2)].reshape(half, TILE)
            give[...] = contract(rows, inverse, 1, 0).astype(jnp.bfloat16)
            give_copy().start()

    row_slots = pl.ds(y * line * 2, line * 2)
    row_tokens = pl.ds(pl.multiple_of(y * (tokens // 2), tokens // 2), tokens // 2)

    def move(token):
        kind = token[0]
        if kind == "d":
            k = int(token[1])
            if k:
                c_direct(k)
            else:
                direct_zero()
        elif kind == "s":
            k = int(token[1])
            if k:
                c_shared(k)
            else:
                shared_zero()
        elif kind == "L":
            line_piece(int(token[1]), int(token[2]), start, True)
        elif kind == "S":
            crossed_piece(int(token[1]), start, True)
        elif kind == "Y":
            crossed_here(start, True)
        elif kind == "P":
            outer_first()

    def moves(stage):
        @pl.when(is_end)
        def _():
            for token in END[stage]:
                move(token)

        @pl.when(jnp.logical_not(is_end))
        def _():
            for token in MIDDLE[stage]:
                move(token)

    moves(0)
    lax.fori_loop(0, groups // 2, c_from_core, 0)
    local.wait()
    gram_rows(0)
    moves(1)
    gram_rows(1)
    scale_c = rounded_factor(gram_c, low_c, tokens)
    moves(2)
    unit_step(0, scale_c)
    moves(3)

    @pl.when(edge == 1)
    def _():
        unit_step(1, scale_c)

    moves(4)

    def more(i, carry):
        for cs in range(2):
            line_piece(i, cs, start, True)
        crossed_piece(i, start, True)
        return carry

    lax.fori_loop(3, line - 1, more, 0)
    row_n = nbuf[row_slots].reshape(tokens // 2, TILE)
    gram_n[...] = contract(row_n, row_n, 0, 0)
    moves(5)

    def pre_in(place):
        unit = place + 3 * p - 4 * block
        inside = jnp.logical_and(unit >= 0, unit <= 3)
        source = jnp.where(edge == 1, unit // 2, unit - 2 * (r - 1))

        @pl.when(jnp.logical_and(inside, source != c))
        def _():
            pre_copy(place, pre_send.at[0], core_peer).wait_recv()

    for place in range(3):
        pre_in(place)
    outer_rest()

    cross[...] = contract(pre[row_tokens, :], nbuf[row_slots].reshape(tokens // 2, TILE), 0, 0)

    def other_row(i, carry):
        zs, _ = line_source(jnp.maximum(i - 1, 0))
        zs = jnp.where(i == 0, z, zs)
        slot = slot_of(1 - y, zs, 0)

        seen = jnp.where(i == 0, is_end, jnp.logical_and(from_end(zs), jnp.logical_not(is_end)))

        @pl.when(jnp.logical_not(seen))
        def _():
            n_to_y(slot).wait_recv()

        n_to_y(slot + 1).wait_recv()
        piece = nbuf[pl.ds(slot, 2)].reshape(2 * tokens_here, TILE)
        gram_n[...] += contract(piece, piece, 0, 0)
        rows = pl.ds(pl.multiple_of(slot * tokens_here, 2 * tokens_here), 2 * tokens_here)
        cross[...] += contract(pre[rows, :], piece, 0, 0)
        return carry

    lax.fori_loop(0, line, other_row, 0)

    pl.semaphore_signal(meet, inc=1, device_id=x_peer, device_id_type=MESH)
    scale_n = rounded_factor(gram_n, low_n, tokens)

    first = contract(cross[...].astype(jnp.bfloat16), low_n[...], 1, 0)
    square = scale_n * scale_n
    cross[...] = (4.0 * scale_n) * cross[...] - (6.0 * square) * first
    second = contract(first.astype(jnp.bfloat16), low_n[...], 1, 0)
    cross[...] += (4.0 * square * scale_n) * second
    second_low[...] = second.astype(jnp.bfloat16)

    def result(h):
        rows = pl.ds(pl.multiple_of(h * strip, strip), strip)
        third = contract(second_low[rows, :], low_n[...], 1, 0)
        return cross[rows, :] - (square * square) * third

    def energy(value):
        total = jnp.sum((value * value).reshape(strip // 8, 8, TILE), axis=0)
        part = total[:, :128]
        for i in range(1, TILE // 128):
            part = part + total[:, i * 128 : (i + 1) * 128]
        return part

    theirs[...] = result(1 - c)
    swap = remote(theirs, arrived, swap_send.at[0], swap_recv.at[0], core_peer)
    swap.start()
    mine[...] = result(c)
    squares[flat] = energy(theirs[...]) + energy(mine[...])

    def sq_copy(d, slot):
        target = (flat + d) % devices
        return remote(
            squares.at[slot],
            squares.at[slot],
            sq_send.at[d],
            sq_recv.at[slot],
            (target // owners, target % owners),
        )

    def sq_start(d, carry):
        sq_copy(d, flat).start()
        return carry

    def sq_wait(d, carry):
        sq_copy(d, (flat + d) % devices).wait_recv()
        return carry

    pl.semaphore_wait(meet, 1)
    lax.fori_loop(1, devices, sq_start, 0)
    lax.fori_loop(1, devices, sq_wait, 0)
    total = jnp.sum(squares[...], axis=0)
    total = jnp.sum(jnp.sum(total, axis=0, keepdims=True), axis=1, keepdims=True)
    final = lax.rsqrt(total / (width * out_width) + 1e-06)
    update_ref[:, pl.ds(pl.multiple_of(c * TILE, TILE), TILE)] = (mine[...] * final).astype(
        jnp.bfloat16
    )
    swap.wait_recv()
    update_ref[:, pl.ds(pl.multiple_of((1 - c) * TILE, TILE), TILE)] = (
        arrived[...] * final
    ).astype(jnp.bfloat16)

    def sq_drain(d, carry):
        sq_copy(d, flat).wait_send()
        return carry

    lax.fori_loop(1, devices, sq_drain, 0)
    swap.wait_send()
    n_pass.wait_send()
    own_out(own_slot, drain)
    own_out(core_slot, drain)

    def line_drain(i, carry):
        for cs in range(2):
            line_piece(i, cs, drain, False)
        crossed_piece(i, drain, False)
        return carry

    lax.fori_loop(0, line - 1, line_drain, 0)
    crossed_here(drain, False)
    c_own.wait_send()

    def c_drain(k):
        slot = c_in_slot(k, 0)
        c_out(k).wait_send()
        c_relay(slot, c_x, x_peer).wait_send()
        c_relay(slot, c_core, core_peer).wait_send()

    def c_shared_drain(k):
        c_relay(c_in_slot(k, 1), c_core, core_peer).wait_send()

    for k in range(1, line):
        c_drain(k)
        c_shared_drain(k)

    @pl.when(x == 1)
    def _():
        c_drain(0)

    @pl.when(x == 0)
    def _():
        c_shared_drain(0)

    def unit_drain(k, carry):
        inside = is_mine(k)

        @pl.when(inside)
        def _():
            pre_copy(place_of(k), pre_send.at[k], core_peer).wait_send()

        @pl.when(jnp.logical_not(inside))
        def _():
            give_copy().wait_send()

        return carry

    lax.fori_loop(0, 1 + edge, unit_drain, 0)
    outer_drain()


def whole(groups, owners, hidden, norm_gain, cotangent):
    tokens_here, width = hidden.shape
    out_width = cotangent.shape[1]
    tokens = groups * tokens_here
    strip = out_width // groups
    line = groups // 4
    low, high = jnp.bfloat16, jnp.float32
    dma = pltpu.SemaphoreType.DMA
    return pl.pallas_call(
        functools.partial(whole_kernel, (groups, owners, tokens_here, width, out_width)),
        out_shape=jax.ShapeDtypeStruct((strip, width // owners), low),
        in_specs=[
            pl.BlockSpec(memory_space=pl.ANY),
            pl.BlockSpec(memory_space=pltpu.VMEM),
            pl.BlockSpec(memory_space=pl.ANY),
        ],
        out_specs=pl.BlockSpec(memory_space=pltpu.VMEM),
        scratch_shapes=[
            pltpu.VMEM((tokens_here, width), low),
            pltpu.VMEM((groups, tokens_here, TILE), low),
            pltpu.VMEM((groups, tokens_here, TILE), low),
            pltpu.VMEM((tokens_here, TILE), low),
            pltpu.VMEM((TILE, TILE), high),
            pltpu.VMEM((TILE, TILE), high),
            pltpu.VMEM((TILE, TILE), low),
            pltpu.VMEM((TILE, TILE), low),
            pltpu.VMEM((tokens, 2 * strip), low),
            pltpu.VMEM((tokens // 2, UNIT), low),
            pltpu.VMEM((2 * strip, TILE), high),
            pltpu.VMEM((2 * strip, TILE), low),
            pltpu.VMEM((strip, TILE), high),
            pltpu.VMEM((strip, TILE), high),
            pltpu.VMEM((strip, TILE), high),
            pltpu.VMEM((groups * owners, 8, 128), high),
            pltpu.SemaphoreType.REGULAR,
            dma((2,)),
            dma((line,)),
            dma((groups,)),
            dma((groups,)),
            dma((groups,)),
            dma((1,)),
            dma((groups,)),
            dma((groups,)),
            dma((groups,)),
            dma((groups,)),
            dma((6,)),
            dma((5,)),
            dma((1,)),
            dma((1,)),
            dma((groups * owners,)),
            dma((groups * owners,)),
        ],
        compiler_params=pltpu.CompilerParams(
            collective_id=0, has_side_effects=True, vmem_limit_bytes=60 * 2**20
        ),
    )(hidden, norm_gain.reshape(1, width), cotangent)


def fits(groups, owners, width, out_width):
    line = groups // 4
    return (
        owners == 2
        and width == 2 * owners * TILE
        and groups % 8 == 0
        and line & (line - 1) == 0
        and line >= 4
        and 8 * out_width == 3 * TILE * groups
    )


def step(hidden, norm_gain, cotangent):
    groups, owners = lax.axis_size("dp"), lax.axis_size("owner")
    if fits(groups, owners, hidden.shape[1], cotangent.shape[1]):
        return whole(groups, owners, hidden, norm_gain, cotangent)
    return shards(hidden, norm_gain, cotangent)


def solution(mesh):
    in_specs = (P("dp", None), P(), P("dp", None))
    out_specs = P("dp", "owner")
    return jax.shard_map(step, mesh=mesh, in_specs=in_specs, out_specs=out_specs, check_vma=False)
```

```python
import functools

import jax
import jax.numpy as jnp
from jax import lax
from jax.experimental import pallas as pl
from jax.experimental.pallas import tpu as pltpu
from jax.sharding import PartitionSpec as P

TILE = 1024


DAMPING = 0.1


def contract(left, right, left_dim, right_dim):
    return lax.dot_general(
        left, right, (((left_dim,), (right_dim,)), ((), ())), preferred_element_type=jnp.float32
    )


def inverse_of(piece, tokens):
    identity = jnp.eye(TILE, dtype=jnp.float32)
    matrix = contract(piece, piece, 0, 0) / tokens + DAMPING * identity
    scale = 1.0 / jnp.max(jnp.sum(jnp.abs(matrix), axis=1))
    first = 2.0 * scale * identity - (scale * scale) * matrix
    first_low = first.astype(jnp.bfloat16)
    matrix_low = matrix.astype(jnp.bfloat16)
    product = contract(first_low, matrix_low, 1, 0).astype(jnp.bfloat16)
    return (2.0 * first - contract(product, first_low, 1, 0)).astype(jnp.bfloat16)


def shards(hidden, norm_gain, cotangent):
    owners = lax.axis_size("owner")
    position = lax.axis_index("owner")
    groups = lax.axis_size("dp")
    group = lax.axis_index("dp")
    tokens_here = hidden.shape[0]
    tokens = tokens_here * groups
    width = hidden.shape[1]
    out_width = cotangent.shape[1]
    strip = out_width // groups
    own = width // owners
    in_width = max(own, TILE)

    firsts = jnp.array([(g * strip) // TILE for g in range(groups)], jnp.int32)
    lasts = jnp.array([((g + 1) * strip - 1) // TILE for g in range(groups)], jnp.int32)
    odd = lax.rem(position, 2) == 1
    wanted = jnp.where(odd, lasts, firsts)
    outgoing = jnp.stack(
        [
            lax.dynamic_slice_in_dim(cotangent, wanted[g] * TILE, TILE, 1)
            for g in range(groups)
        ]
    )
    out_piece = lax.all_to_all(outgoing, "dp", 0, 0, tiled=True).reshape(tokens, TILE)

    states = hidden.astype(jnp.float32)
    normed = (
        states * lax.rsqrt(jnp.mean(states * states, axis=1, keepdims=True) + 1e-05) * norm_gain
    ).astype(jnp.bfloat16)
    in_start = (position * own) // TILE * TILE
    mine = lax.dynamic_slice_in_dim(normed, in_start, in_width, 1)
    in_piece = lax.all_gather(mine, "dp", axis=0, tiled=True)

    out_inverse = inverse_of(out_piece, tokens)
    padded = jnp.pad(out_inverse, ((0, 0), (strip, strip)))
    offset = group * strip - wanted[group] * TILE
    strip_inverse = lax.dynamic_slice_in_dim(padded, offset + strip, strip, 1)
    part = contract(out_piece, strip_inverse, 1, 0).astype(jnp.bfloat16)
    other = lax.ppermute(part, "owner", [(o, o ^ 1) for o in range(owners)])
    column_block = (group * strip + jnp.arange(strip, dtype=jnp.int32)) // TILE
    pre_out = jnp.where((column_block == wanted[group])[None, :], part, other)

    results = []
    for block in range(in_width // TILE):
        piece = in_piece[:, block * TILE : (block + 1) * TILE]
        inverse = inverse_of(piece, tokens)
        if own < TILE:
            inverse = lax.dynamic_slice_in_dim(inverse, position * own - in_start, own, 1)
        cross = contract(pre_out, piece, 0, 0).astype(jnp.bfloat16)
        results.append(contract(cross, inverse, 1, 0))
    summed = jnp.concatenate(results, axis=1)
    squares = lax.psum(jnp.sum(summed * summed), ("dp", "owner"))
    return (summed * lax.rsqrt(squares / (width * out_width) + 1e-06)).astype(jnp.bfloat16)


MESH = pl.DeviceIdType.MESH
UNIT = TILE // 4
CHUNK = 128
EARLY = (1, 2, 3)
MIDDLE = (
    ("d0", "d2", "d1", "s2", "L10", "s0", "d3", "L00", "s1", "L11", "L01", "s3",),
    (),
    ("L20", "S0",),
    ("L21",),
    (),
    ("Y", "S1", "P", "S2",),
)
END = (
    ("d1", "S2", "s1", "s0", "d0", "S0", "d2", "Y", "d3", "L00", "s3", "L01", "s2",),
    ("L10",),
    (),
    ("S1", "L20",),
    ("P", "L11", "L21",),
    (),
)


def flipped(value, mask):
    for bit in range(mask.bit_length()):
        if (mask >> bit) & 1:
            value = value + (1 - 2 * ((value // 2**bit) % 2)) * 2**bit
    return value


def rounded_factor(gram, low, tokens):
    row = lax.broadcasted_iota(jnp.int32, (CHUNK, CHUNK), 0)
    column = lax.broadcasted_iota(jnp.int32, (CHUNK, CHUNK), 1)
    damping = jnp.where(row == column, DAMPING, 0.0)

    def put(i, total):
        rows = pl.ds(pl.multiple_of(i * CHUNK, CHUNK), CHUNK)
        matrix = gram[rows, :] * (1.0 / tokens)
        low[rows, :] = matrix.astype(jnp.bfloat16)
        low[rows, rows] = (gram[rows, rows] * (1.0 / tokens) + damping).astype(jnp.bfloat16)
        folded = jnp.sum(jnp.abs(matrix).reshape(CHUNK // 8, 8, TILE), axis=0)
        return total + folded

    sums = lax.fori_loop(0, TILE // CHUNK, put, jnp.zeros((8, TILE), jnp.float32))
    sums = jnp.sum(sums, axis=0, keepdims=True)
    return 1.0 / (jnp.max(sums, axis=1, keepdims=True) + DAMPING)


def whole_kernel(
    sizes,
    hidden_ref,
    gain_ref,
    cotangent_ref,
    update_ref,
    states,
    cbuf,
    nbuf,
    other_n,
    gram_c,
    gram_n,
    low_c,
    low_n,
    pre,
    give,
    cross,
    first_low,
    second_low,
    mine,
    theirs,
    arrived,
    squares,
    put_low,
    put_sem,
    meet,
    load_sem,
    c_send,
    c_x,
    c_core,
    c_recv,
    n_core,
    n_up,
    n_down,
    n_y,
    n_recv,
    pre_send,
    pre_recv,
    swap_send,
    swap_recv,
    sq_send,
    sq_recv,
):
    groups, owners, tokens_here, width, out_width = sizes
    tokens = groups * tokens_here
    line = groups // 4
    strip = out_width // groups
    own = width // owners
    me = lax.axis_index("dp")
    x = lax.axis_index("owner")
    z = me // 4
    y = (me // 2) % 2
    c = me % 2
    devices = groups * owners
    flat = me * owners + x

    def slot_of(y_, z_, c_):
        return (y_ * line + z_) * 2 + c_

    def device(x_, y_, z_, c_):
        return ((z_ * 2 + y_) * 2 + c_, x_)

    def block_of(p):
        return 3 * (p // 4) + (p % 4 + 1) // 2

    def remote(src, dst, send, recv, target):
        return pltpu.make_async_remote_copy(
            src_ref=src,
            dst_ref=dst,
            send_sem=send,
            recv_sem=recv,
            device_id=target,
            device_id_type=MESH,
        )

    own_slot = slot_of(y, z, c)
    core_slot = slot_of(y, z, 1 - c)
    core_peer = device(x, y, z, 1 - c)
    x_peer = device(1 - x, y, z, c)

    load = pltpu.make_async_copy(hidden_ref, states, load_sem.at[0])
    load.start()

    barrier = pltpu.get_barrier_semaphore()

    def greet(target):
        pl.semaphore_signal(barrier, inc=1, device_id=target, device_id_type=MESH)

    greet(core_peer)
    greet(x_peer)
    greet(device(x, 1 - y, z, c))
    for k in range(1, line):
        zd = flipped(z, k)
        greet(device(x, (y + x + z + zd) % 2, zd, c))

    @pl.when(z + 1 < line)
    def _():
        greet(device(x, y, z + 1, c))

    @pl.when(z > 0)
    def _():
        greet(device(x, y, z - 1, c))

    pl.semaphore_wait(barrier, 2 + line + jnp.where(z + 1 < line, 1, 0) + jnp.where(z > 0, 1, 0))

    def block_columns(y_, z_):
        return pl.ds(pl.multiple_of(block_of(z_ * 2 + y_) * TILE, TILE), TILE)

    def c_out(k):
        zd = flipped(z, k)
        yd = (y + x + z + zd) % 2
        return remote(
            cotangent_ref.at[:, block_columns(yd, zd)],
            cbuf.at[own_slot],
            c_send.at[k],
            c_recv.at[own_slot],
            device(x, yd, zd, c),
        )

    def c_in_slot(k, through):
        zs = flipped(z, k)
        ys = (y + x + through + z + zs) % 2
        return slot_of(ys, zs, c)

    def c_relay(slot, sems, target):
        return remote(cbuf.at[slot], cbuf.at[slot], sems.at[slot], c_recv.at[slot], target)

    early = EARLY
    for k in early:
        c_out(k).start()

    @pl.when(x == 1)
    def _():
        c_out(0).start()

    local = pltpu.make_async_copy(
        cotangent_ref.at[:, block_columns(y, z)], cbuf.at[own_slot], load_sem.at[1]
    )
    local.start()
    c_own = remote(
        cotangent_ref.at[:, block_columns(y, z)],
        cbuf.at[own_slot],
        c_core.at[own_slot],
        c_recv.at[own_slot],
        core_peer,
    )
    c_own.start()

    load.wait()
    part = 16
    kept = pl.ds(pl.multiple_of(x * own + c * TILE, TILE), TILE)
    passed = pl.ds(pl.multiple_of(x * own + (1 - c) * TILE, TILE), TILE)

    def normalize(i, carry):
        rows = pl.ds(pl.multiple_of(i * part, part), part)
        full = states[rows, :].astype(jnp.float32)
        factor = lax.rsqrt(jnp.sum(full * full, axis=1, keepdims=True) * (1.0 / width) + 1e-05)
        for columns, put in ((passed, other_n), (kept, nbuf.at[own_slot])):
            piece = states[rows, columns].astype(jnp.float32) * factor * gain_ref[:, columns]
            put[rows, :] = piece.astype(jnp.bfloat16)
        return carry

    lax.fori_loop(0, tokens_here // part, normalize, 0)
    n_pass = remote(other_n, nbuf.at[own_slot], n_core.at[0], n_recv.at[own_slot], core_peer)
    n_pass.start()

    def n_copy(slot, sems, target):
        return remote(nbuf.at[slot], nbuf.at[slot], sems.at[slot], n_recv.at[slot], target)

    def n_to_y(slot):
        return n_copy(slot, n_y, device(x, 1 - y, z, c))

    def n_to_up(slot):
        return n_copy(slot, n_up, device(x, y, z + 1, c))

    def n_to_down(slot):
        return n_copy(slot, n_down, device(x, y, z - 1, c))

    def own_out(slot, act):
        act(n_to_y(slot))

        @pl.when(z + 1 < line)
        def _():
            act(n_to_up(slot))

        @pl.when(z > 0)
        def _():
            act(n_to_down(slot))

    def start(copy):
        copy.start()

    def drain(copy):
        copy.wait_send()

    own_out(own_slot, start)
    n_to_y(core_slot).wait_recv()
    own_out(core_slot, start)
    for k in range(1, line):
        if k not in early:
            c_out(k).start()

    def line_source(i):
        low = jnp.minimum(z, line - 1 - z)
        near = i < 2 * low
        distance = jnp.where(near, i // 2 + 1, i + 1 - low)
        below = jnp.where(near, i % 2 == 0, z > low)
        return jnp.where(below, z - distance, z + distance), below

    def line_out(slot, below, act):
        @pl.when(jnp.logical_and(below, z + 1 < line))
        def _():
            act(n_to_up(slot))

        @pl.when(jnp.logical_and(jnp.logical_not(below), z > 0))
        def _():
            act(n_to_down(slot))

    is_end = jnp.logical_or(z == 0, z == line - 1)

    def from_end(zs):
        return jnp.logical_or(zs == 0, zs == line - 1)

    def line_piece(i, cs, act, wait):
        zs, below = line_source(i)
        slot = slot_of(y, zs, cs)
        if wait:
            n_to_y(slot).wait_recv()
        line_out(slot, below, act)
        if cs == 0:

            @pl.when(jnp.logical_not(from_end(zs)))
            def _():
                act(n_to_y(slot))
        else:
            act(n_to_y(slot))

    def crossed_piece(i, act, wait):
        zs, below = line_source(i)

        @pl.when(jnp.logical_and(from_end(zs), jnp.logical_not(is_end)))
        def _():
            slot = slot_of(1 - y, zs, 0)
            if wait:
                n_to_y(slot).wait_recv()
            line_out(slot, below, act)

    def crossed_here(act, wait):
        @pl.when(is_end)
        def _():
            slot = slot_of(1 - y, z, 0)
            if wait:
                n_to_y(slot).wait_recv()
            line_out(slot, z == 0, act)

    def c_direct(k):
        slot = c_in_slot(k, 0)
        c_relay(slot, c_x, x_peer).wait_recv()
        c_relay(slot, c_x, x_peer).start()
        c_relay(slot, c_core, core_peer).start()

    def c_from_core(i, carry):
        slot = 2 * i + 1 - c
        c_relay(slot, c_core, core_peer).wait_recv()
        return carry

    def direct_zero():
        @pl.when(x == 1)
        def _():
            c_direct(0)

    def c_shared(k):
        slot = c_in_slot(k, 1)
        c_relay(slot, c_core, core_peer).wait_recv()
        c_relay(slot, c_core, core_peer).start()

    def shared_zero():
        @pl.when(x == 0)
        def _():
            c_shared(0)

    def gram_rows(i):
        block_tokens = cbuf[...].reshape(tokens, TILE)
        part = slice(i * TILE // 2, (i + 1) * TILE // 2)
        gram_c[part, :] = contract(block_tokens[:, part], block_tokens, 0, 0)

    p = z * 2 + y
    r = p % 4
    edge = jnp.where(jnp.logical_or(r == 0, r == 3), 1, 0)
    block = block_of(p)

    def unit_of(k):
        return edge * (3 * c + k * (1 - 2 * c)) + (1 - edge) * (2 * (r - 1) + c)

    def place_of(k):
        return 4 * block + unit_of(k) - 3 * p

    def strip_columns(place):
        return pl.ds(pl.multiple_of(place * UNIT, UNIT), UNIT)

    def pre_copy(place, send, target):
        view = pre.at[:, strip_columns(place)]
        return remote(view, view, send, pre_recv.at[place], target)

    half = tokens // 2

    def half_rows(h):
        return pl.ds(pl.multiple_of(h * half, half), half)

    def give_copy():
        place = place_of(0) - 3 * (1 - 2 * y)
        return remote(
            give,
            pre.at[half_rows(x), strip_columns(place)],
            pre_send.at[2],
            pre_recv.at[3 + x],
            device(x, 1 - y, z, c),
        )

    outer_place = (r - 1) * 2

    def outer_copy(h, send, target):
        view = pre.at[half_rows(h), strip_columns(outer_place)]
        return remote(view, view, pre_send.at[send], pre_recv.at[3 + h], target)

    def outer_first():
        @pl.when(jnp.logical_and(edge == 0, c == 2 - r))
        def _():
            outer_copy(x, 3, x_peer).wait_recv()
            outer_copy(x, 3, x_peer).start()
            outer_copy(x, 4, core_peer).start()

    def outer_rest():
        @pl.when(jnp.logical_and(edge == 0, c == 2 - r))
        def _():
            outer_copy(1 - x, 5, core_peer).wait_recv()
            outer_copy(1 - x, 5, core_peer).start()

        @pl.when(jnp.logical_and(edge == 0, c == r - 1))
        def _():
            outer_copy(0, 3, core_peer).wait_recv()
            outer_copy(1, 3, core_peer).wait_recv()

    def outer_drain():
        @pl.when(jnp.logical_and(edge == 0, c == 2 - r))
        def _():
            outer_copy(x, 3, x_peer).wait_send()
            outer_copy(x, 4, core_peer).wait_send()
            outer_copy(1 - x, 5, core_peer).wait_send()

    def unit_inverse(k, scale_c):
        unit = unit_of(k)
        first = low_c[:, pl.ds(pl.multiple_of(unit * UNIT, UNIT), UNIT)]
        second = contract(low_c[...], first, 1, 0)
        third = contract(low_c[...], second.astype(jnp.bfloat16), 1, 0)
        row = lax.broadcasted_iota(jnp.int32, (TILE, UNIT), 0)
        column = lax.broadcasted_iota(jnp.int32, (TILE, UNIT), 1) + unit * UNIT
        start4 = jnp.where(row == column, 4.0, 0.0)
        powers = [scale_c, scale_c**2, scale_c**3, scale_c**4]
        inverse = powers[0] * start4 - (6.0 * powers[1]) * first.astype(jnp.float32)
        inverse = inverse + (4.0 * powers[2]) * second - powers[3] * third
        return inverse.astype(jnp.bfloat16)

    def is_mine(k):
        place = place_of(k)
        return jnp.logical_and(place >= 0, place < 3)

    def unit_step(k, scale_c):
        inverse = unit_inverse(k, scale_c)
        inside = is_mine(k)

        @pl.when(inside)
        def _():
            whole = cbuf[...].reshape(tokens, TILE)
            pre[:, strip_columns(place_of(k))] = contract(whole, inverse, 1, 0).astype(jnp.bfloat16)
            pre_copy(place_of(k), pre_send.at[k], core_peer).start()

        @pl.when(jnp.logical_not(inside))
        def _():
            rows = cbuf[pl.ds(x * (groups // 2), groups // 2)].reshape(half, TILE)
            give[...] = contract(rows, inverse, 1, 0).astype(jnp.bfloat16)
            give_copy().start()

    row_slots = pl.ds(y * line * 2, line * 2)
    row_tokens = pl.ds(pl.multiple_of(y * (tokens // 2), tokens // 2), tokens // 2)

    def move(token):
        kind = token[0]
        if kind == "d":
            k = int(token[1])
            if k:
                c_direct(k)
            else:
                direct_zero()
        elif kind == "s":
            k = int(token[1])
            if k:
                c_shared(k)
            else:
                shared_zero()
        elif kind == "L":
            line_piece(int(token[1]), int(token[2]), start, True)
        elif kind == "S":
            crossed_piece(int(token[1]), start, True)
        elif kind == "Y":
            crossed_here(start, True)
        elif kind == "P":
            outer_first()

    def moves(stage):
        @pl.when(is_end)
        def _():
            for token in END[stage]:
                move(token)

        @pl.when(jnp.logical_not(is_end))
        def _():
            for token in MIDDLE[stage]:
                move(token)

    moves(0)
    lax.fori_loop(0, groups // 2, c_from_core, 0)
    local.wait()
    gram_rows(0)
    moves(1)
    gram_rows(1)
    scale_c = rounded_factor(gram_c, low_c, tokens)
    moves(2)
    unit_step(0, scale_c)
    moves(3)

    @pl.when(edge == 1)
    def _():
        unit_step(1, scale_c)

    moves(4)

    def more(i, carry):
        for cs in range(2):
            line_piece(i, cs, start, True)
        crossed_piece(i, start, True)
        return carry

    lax.fori_loop(3, line - 1, more, 0)
    row_n = nbuf[row_slots].reshape(tokens // 2, TILE)
    gram_n[...] = contract(row_n, row_n, 0, 0)
    moves(5)

    def pre_in(place):
        unit = place + 3 * p - 4 * block
        inside = jnp.logical_and(unit >= 0, unit <= 3)
        source = jnp.where(edge == 1, unit // 2, unit - 2 * (r - 1))

        @pl.when(jnp.logical_and(inside, source != c))
        def _():
            pre_copy(place, pre_send.at[0], core_peer).wait_recv()

    for place in range(3):
        pre_in(place)
    outer_rest()

    cross[...] = contract(pre[row_tokens, :], nbuf[row_slots].reshape(tokens // 2, TILE), 0, 0)

    def other_row(i, carry):
        zs, _ = line_source(jnp.maximum(i - 1, 0))
        zs = jnp.where(i == 0, z, zs)
        slot = slot_of(1 - y, zs, 0)

        seen = jnp.where(i == 0, is_end, jnp.logical_and(from_end(zs), jnp.logical_not(is_end)))

        @pl.when(jnp.logical_not(seen))
        def _():
            n_to_y(slot).wait_recv()

        n_to_y(slot + 1).wait_recv()
        piece = nbuf[pl.ds(slot, 2)].reshape(2 * tokens_here, TILE)
        gram_n[...] += contract(piece, piece, 0, 0)
        rows = pl.ds(pl.multiple_of(slot * tokens_here, 2 * tokens_here), 2 * tokens_here)
        cross[...] += contract(pre[rows, :], piece, 0, 0)
        return carry

    lax.fori_loop(0, line, other_row, 0)

    pl.semaphore_signal(meet, inc=1, device_id=x_peer, device_id_type=MESH)
    scale_n = rounded_factor(gram_n, low_n, tokens)

    square = scale_n * scale_n
    first = contract(cross[...].astype(jnp.bfloat16), low_n[...], 1, 0)
    first_low[...] = first.astype(jnp.bfloat16)
    cross[...] = (4.0 * scale_n) * cross[...] - (6.0 * square) * first
    second_low[...] = contract(first_low[...], low_n[...], 1, 0).astype(jnp.bfloat16)

    def result(h):
        rows = pl.ds(pl.multiple_of(h * strip, strip), strip)
        second = second_low[rows, :]
        third = contract(second, low_n[...], 1, 0)
        partial = cross[rows, :] + (4.0 * square * scale_n) * second.astype(jnp.float32)
        return partial - (square * square) * third

    def energy(value):
        total = jnp.sum((value * value).reshape(strip // 8, 8, TILE), axis=0)
        part = total[:, :128]
        for i in range(1, TILE // 128):
            part = part + total[:, i * 128 : (i + 1) * 128]
        return part

    theirs[...] = result(1 - c)
    swap = remote(theirs, arrived, swap_send.at[0], swap_recv.at[0], core_peer)
    swap.start()
    mine[...] = result(c)
    squares[flat] = energy(theirs[...]) + energy(mine[...])

    def sq_copy(d, slot):
        target = (flat + d) % devices
        return remote(
            squares.at[slot],
            squares.at[slot],
            sq_send.at[d],
            sq_recv.at[slot],
            (target // owners, target % owners),
        )

    def sq_start(d, carry):
        sq_copy(d, flat).start()
        return carry

    def sq_wait(d, carry):
        sq_copy(d, (flat + d) % devices).wait_recv()
        sq_copy(d, flat).wait_send()
        return carry

    pl.semaphore_wait(meet, 1)
    lax.fori_loop(1, devices, sq_start, 0)
    n_pass.wait_send()
    own_out(own_slot, drain)
    own_out(core_slot, drain)

    def line_drain(i, carry):
        for cs in range(2):
            line_piece(i, cs, drain, False)
        crossed_piece(i, drain, False)
        return carry

    lax.fori_loop(0, line - 1, line_drain, 0)
    crossed_here(drain, False)
    c_own.wait_send()

    def c_drain(k):
        slot = c_in_slot(k, 0)
        c_out(k).wait_send()
        c_relay(slot, c_x, x_peer).wait_send()
        c_relay(slot, c_core, core_peer).wait_send()

    def c_shared_drain(k):
        c_relay(c_in_slot(k, 1), c_core, core_peer).wait_send()

    for k in range(1, line):
        c_drain(k)
        c_shared_drain(k)

    @pl.when(x == 1)
    def _():
        c_drain(0)

    @pl.when(x == 0)
    def _():
        c_shared_drain(0)

    def unit_drain(k, carry):
        inside = is_mine(k)

        @pl.when(inside)
        def _():
            pre_copy(place_of(k), pre_send.at[k], core_peer).wait_send()

        @pl.when(jnp.logical_not(inside))
        def _():
            give_copy().wait_send()

        return carry

    lax.fori_loop(0, 1 + edge, unit_drain, 0)
    outer_drain()
    swap.wait()
    lax.fori_loop(1, devices, sq_wait, 0)
    total = jnp.sum(squares[...], axis=0)
    total = jnp.sum(jnp.sum(total, axis=0, keepdims=True), axis=1, keepdims=True)
    final = lax.rsqrt(total / (width * out_width) + 1e-06)

    def put(half, value, h):
        put_low[half] = (value * final).astype(jnp.bfloat16)
        columns = pl.ds(pl.multiple_of(h * TILE, TILE), TILE)
        copy = pltpu.make_async_copy(
            put_low.at[half], update_ref.at[:, columns], put_sem.at[half]
        )
        copy.start()
        return copy

    first_put = put(0, mine[...], c)
    second_put = put(1, arrived[...], 1 - c)
    first_put.wait()
    second_put.wait()


def whole(groups, owners, hidden, norm_gain, cotangent):
    tokens_here, width = hidden.shape
    out_width = cotangent.shape[1]
    tokens = groups * tokens_here
    strip = out_width // groups
    line = groups // 4
    low, high = jnp.bfloat16, jnp.float32
    dma = pltpu.SemaphoreType.DMA
    return pl.pallas_call(
        functools.partial(whole_kernel, (groups, owners, tokens_here, width, out_width)),
        out_shape=jax.ShapeDtypeStruct((strip, width // owners), low),
        in_specs=[
            pl.BlockSpec(memory_space=pl.ANY),
            pl.BlockSpec(memory_space=pltpu.VMEM),
            pl.BlockSpec(memory_space=pl.ANY),
        ],
        out_specs=pl.BlockSpec(memory_space=pl.ANY),
        scratch_shapes=[
            pltpu.VMEM((tokens_here, width), low),
            pltpu.VMEM((groups, tokens_here, TILE), low),
            pltpu.VMEM((groups, tokens_here, TILE), low),
            pltpu.VMEM((tokens_here, TILE), low),
            pltpu.VMEM((TILE, TILE), high),
            pltpu.VMEM((TILE, TILE), high),
            pltpu.VMEM((TILE, TILE), low),
            pltpu.VMEM((TILE, TILE), low),
            pltpu.VMEM((tokens, 2 * strip), low),
            pltpu.VMEM((tokens // 2, UNIT), low),
            pltpu.VMEM((2 * strip, TILE), high),
            pltpu.VMEM((2 * strip, TILE), low),
            pltpu.VMEM((2 * strip, TILE), low),
            pltpu.VMEM((strip, TILE), high),
            pltpu.VMEM((strip, TILE), high),
            pltpu.VMEM((strip, TILE), high),
            pltpu.VMEM((groups * owners, 8, 128), high),
            pltpu.VMEM((2, strip, TILE), low),
            dma((2,)),
            pltpu.SemaphoreType.REGULAR,
            dma((2,)),
            dma((line,)),
            dma((groups,)),
            dma((groups,)),
            dma((groups,)),
            dma((1,)),
            dma((groups,)),
            dma((groups,)),
            dma((groups,)),
            dma((groups,)),
            dma((6,)),
            dma((5,)),
            dma((1,)),
            dma((1,)),
            dma((groups * owners,)),
            dma((groups * owners,)),
        ],
        compiler_params=pltpu.CompilerParams(
            collective_id=0, has_side_effects=True, vmem_limit_bytes=60 * 2**20
        ),
    )(hidden, norm_gain.reshape(1, width), cotangent)


def fits(groups, owners, width, out_width):
    line = groups // 4
    return (
        owners == 2
        and width == 2 * owners * TILE
        and groups % 8 == 0
        and line & (line - 1) == 0
        and line >= 4
        and 8 * out_width == 3 * TILE * groups
    )


def step(hidden, norm_gain, cotangent):
    groups, owners = lax.axis_size("dp"), lax.axis_size("owner")
    if fits(groups, owners, hidden.shape[1], cotangent.shape[1]):
        return whole(groups, owners, hidden, norm_gain, cotangent)
    return shards(hidden, norm_gain, cotangent)


def solution(mesh):
    in_specs = (P("dp", None), P(), P("dp", None))
    out_specs = P("dp", "owner")
    return jax.shard_map(step, mesh=mesh, in_specs=in_specs, out_specs=out_specs, check_vma=False)
```

```python
import functools

import jax
import jax.numpy as jnp
from jax import lax
from jax.experimental import pallas as pl
from jax.experimental.pallas import tpu as pltpu
from jax.sharding import PartitionSpec as P

TILE = 1024


DAMPING = 0.1


def contract(left, right, left_dim, right_dim):
    return lax.dot_general(
        left, right, (((left_dim,), (right_dim,)), ((), ())), preferred_element_type=jnp.float32
    )


def inverse_of(piece, tokens):
    identity = jnp.eye(TILE, dtype=jnp.float32)
    matrix = contract(piece, piece, 0, 0) / tokens + DAMPING * identity
    scale = 1.0 / jnp.max(jnp.sum(jnp.abs(matrix), axis=1))
    first = 2.0 * scale * identity - (scale * scale) * matrix
    first_low = first.astype(jnp.bfloat16)
    matrix_low = matrix.astype(jnp.bfloat16)
    product = contract(first_low, matrix_low, 1, 0).astype(jnp.bfloat16)
    return (2.0 * first - contract(product, first_low, 1, 0)).astype(jnp.bfloat16)


def shards(hidden, norm_gain, cotangent):
    owners = lax.axis_size("owner")
    position = lax.axis_index("owner")
    groups = lax.axis_size("dp")
    group = lax.axis_index("dp")
    tokens_here = hidden.shape[0]
    tokens = tokens_here * groups
    width = hidden.shape[1]
    out_width = cotangent.shape[1]
    strip = out_width // groups
    own = width // owners
    in_width = max(own, TILE)

    firsts = jnp.array([(g * strip) // TILE for g in range(groups)], jnp.int32)
    lasts = jnp.array([((g + 1) * strip - 1) // TILE for g in range(groups)], jnp.int32)
    odd = lax.rem(position, 2) == 1
    wanted = jnp.where(odd, lasts, firsts)
    outgoing = jnp.stack(
        [
            lax.dynamic_slice_in_dim(cotangent, wanted[g] * TILE, TILE, 1)
            for g in range(groups)
        ]
    )
    out_piece = lax.all_to_all(outgoing, "dp", 0, 0, tiled=True).reshape(tokens, TILE)

    states = hidden.astype(jnp.float32)
    normed = (
        states * lax.rsqrt(jnp.mean(states * states, axis=1, keepdims=True) + 1e-05) * norm_gain
    ).astype(jnp.bfloat16)
    in_start = (position * own) // TILE * TILE
    mine = lax.dynamic_slice_in_dim(normed, in_start, in_width, 1)
    in_piece = lax.all_gather(mine, "dp", axis=0, tiled=True)

    out_inverse = inverse_of(out_piece, tokens)
    padded = jnp.pad(out_inverse, ((0, 0), (strip, strip)))
    offset = group * strip - wanted[group] * TILE
    strip_inverse = lax.dynamic_slice_in_dim(padded, offset + strip, strip, 1)
    part = contract(out_piece, strip_inverse, 1, 0).astype(jnp.bfloat16)
    other = lax.ppermute(part, "owner", [(o, o ^ 1) for o in range(owners)])
    column_block = (group * strip + jnp.arange(strip, dtype=jnp.int32)) // TILE
    pre_out = jnp.where((column_block == wanted[group])[None, :], part, other)

    results = []
    for block in range(in_width // TILE):
        piece = in_piece[:, block * TILE : (block + 1) * TILE]
        inverse = inverse_of(piece, tokens)
        if own < TILE:
            inverse = lax.dynamic_slice_in_dim(inverse, position * own - in_start, own, 1)
        cross = contract(pre_out, piece, 0, 0).astype(jnp.bfloat16)
        results.append(contract(cross, inverse, 1, 0))
    summed = jnp.concatenate(results, axis=1)
    squares = lax.psum(jnp.sum(summed * summed), ("dp", "owner"))
    return (summed * lax.rsqrt(squares / (width * out_width) + 1e-06)).astype(jnp.bfloat16)


MESH = pl.DeviceIdType.MESH
UNIT = TILE // 4
CHUNK = 128
EARLY = (1, 2, 3)
MIDDLE = (
    ("d0", "d2", "d1", "s2", "L10", "s0", "d3", "L00", "s1", "L11", "L01", "s3",),
    (),
    ("L20", "S0",),
    ("L21",),
    (),
    ("Y", "S1", "P", "S2",),
)
END = (
    ("d1", "S2", "s1", "s0", "d0", "S0", "d2", "Y", "d3", "L00", "s3", "L01", "s2",),
    ("L10",),
    (),
    ("S1", "L20",),
    ("P", "L11", "L21",),
    (),
)


def flipped(value, mask):
    for bit in range(mask.bit_length()):
        if (mask >> bit) & 1:
            value = value + (1 - 2 * ((value // 2**bit) % 2)) * 2**bit
    return value


def rounded_factor(gram, low, tokens):
    row = lax.broadcasted_iota(jnp.int32, (CHUNK, CHUNK), 0)
    column = lax.broadcasted_iota(jnp.int32, (CHUNK, CHUNK), 1)
    damping = jnp.where(row == column, DAMPING, 0.0)

    def put(i, total):
        rows = pl.ds(pl.multiple_of(i * CHUNK, CHUNK), CHUNK)
        matrix = gram[rows, :] * (1.0 / tokens)
        low[rows, :] = matrix.astype(jnp.bfloat16)
        low[rows, rows] = (gram[rows, rows] * (1.0 / tokens) + damping).astype(jnp.bfloat16)
        folded = jnp.sum(jnp.abs(matrix).reshape(CHUNK // 8, 8, TILE), axis=0)
        return total + folded

    sums = lax.fori_loop(0, TILE // CHUNK, put, jnp.zeros((8, TILE), jnp.float32))
    sums = jnp.sum(sums, axis=0, keepdims=True)
    return 1.0 / (jnp.max(sums, axis=1, keepdims=True) + DAMPING)


def whole_kernel(
    sizes,
    hidden_ref,
    gain_ref,
    cotangent_ref,
    update_ref,
    states,
    cbuf,
    nbuf,
    other_n,
    gram_c,
    gram_n,
    low_c,
    low_n,
    pre,
    give,
    cross,
    first_low,
    second_low,
    mine,
    theirs,
    arrived,
    squares,
    put_low,
    put_sem,
    meet,
    load_sem,
    c_send,
    c_x,
    c_core,
    c_recv,
    n_core,
    n_up,
    n_down,
    n_y,
    n_recv,
    pre_send,
    pre_recv,
    swap_send,
    swap_recv,
    sq_send,
    sq_recv,
):
    groups, owners, tokens_here, width, out_width = sizes
    tokens = groups * tokens_here
    line = groups // 4
    strip = out_width // groups
    own = width // owners
    me = lax.axis_index("dp")
    x = lax.axis_index("owner")
    z = me // 4
    y = (me // 2) % 2
    c = me % 2
    devices = groups * owners
    flat = me * owners + x

    def slot_of(y_, z_, c_):
        return (y_ * line + z_) * 2 + c_

    def device(x_, y_, z_, c_):
        return ((z_ * 2 + y_) * 2 + c_, x_)

    def block_of(p):
        return 3 * (p // 4) + (p % 4 + 1) // 2

    def remote(src, dst, send, recv, target):
        return pltpu.make_async_remote_copy(
            src_ref=src,
            dst_ref=dst,
            send_sem=send,
            recv_sem=recv,
            device_id=target,
            device_id_type=MESH,
        )

    own_slot = slot_of(y, z, c)
    core_slot = slot_of(y, z, 1 - c)
    core_peer = device(x, y, z, 1 - c)
    x_peer = device(1 - x, y, z, c)

    load = pltpu.make_async_copy(hidden_ref, states, load_sem.at[0])
    load.start()

    barrier = pltpu.get_barrier_semaphore()

    def greet(target):
        pl.semaphore_signal(barrier, inc=1, device_id=target, device_id_type=MESH)

    greet(core_peer)
    greet(x_peer)
    greet(device(x, 1 - y, z, c))
    for k in range(1, line):
        zd = flipped(z, k)
        greet(device(x, (y + x + z + zd) % 2, zd, c))

    @pl.when(z + 1 < line)
    def _():
        greet(device(x, y, z + 1, c))

    @pl.when(z > 0)
    def _():
        greet(device(x, y, z - 1, c))

    pl.semaphore_wait(barrier, 2 + line + jnp.where(z + 1 < line, 1, 0) + jnp.where(z > 0, 1, 0))

    def block_columns(y_, z_):
        return pl.ds(pl.multiple_of(block_of(z_ * 2 + y_) * TILE, TILE), TILE)

    def c_out(k):
        zd = flipped(z, k)
        yd = (y + x + z + zd) % 2
        return remote(
            cotangent_ref.at[:, block_columns(yd, zd)],
            cbuf.at[own_slot],
            c_send.at[k],
            c_recv.at[own_slot],
            device(x, yd, zd, c),
        )

    def c_in_slot(k, through):
        zs = flipped(z, k)
        ys = (y + x + through + z + zs) % 2
        return slot_of(ys, zs, c)

    def c_relay(slot, sems, target):
        return remote(cbuf.at[slot], cbuf.at[slot], sems.at[slot], c_recv.at[slot], target)

    early = EARLY
    for k in early:
        c_out(k).start()

    @pl.when(x == 1)
    def _():
        c_out(0).start()

    local = pltpu.make_async_copy(
        cotangent_ref.at[:, block_columns(y, z)], cbuf.at[own_slot], load_sem.at[1]
    )
    local.start()
    c_own = remote(
        cotangent_ref.at[:, block_columns(y, z)],
        cbuf.at[own_slot],
        c_core.at[own_slot],
        c_recv.at[own_slot],
        core_peer,
    )
    c_own.start()

    load.wait()
    part = 32
    kept = pl.ds(pl.multiple_of(x * own + c * TILE, TILE), TILE)
    passed = pl.ds(pl.multiple_of(x * own + (1 - c) * TILE, TILE), TILE)

    def normalize(i, carry):
        rows = pl.ds(pl.multiple_of(i * part, part), part)
        full = states[rows, :].astype(jnp.float32)
        factor = lax.rsqrt(jnp.sum(full * full, axis=1, keepdims=True) * (1.0 / width) + 1e-05)
        for columns, put in ((passed, other_n), (kept, nbuf.at[own_slot])):
            piece = states[rows, columns].astype(jnp.float32) * factor * gain_ref[:, columns]
            put[rows, :] = piece.astype(jnp.bfloat16)
        return carry

    lax.fori_loop(0, tokens_here // part, normalize, 0)
    n_pass = remote(other_n, nbuf.at[own_slot], n_core.at[0], n_recv.at[own_slot], core_peer)
    n_pass.start()

    def n_copy(slot, sems, target):
        return remote(nbuf.at[slot], nbuf.at[slot], sems.at[slot], n_recv.at[slot], target)

    def n_to_y(slot):
        return n_copy(slot, n_y, device(x, 1 - y, z, c))

    def n_to_up(slot):
        return n_copy(slot, n_up, device(x, y, z + 1, c))

    def n_to_down(slot):
        return n_copy(slot, n_down, device(x, y, z - 1, c))

    def own_out(slot, act):
        act(n_to_y(slot))

        @pl.when(z + 1 < line)
        def _():
            act(n_to_up(slot))

        @pl.when(z > 0)
        def _():
            act(n_to_down(slot))

    def start(copy):
        copy.start()

    def drain(copy):
        copy.wait_send()

    own_out(own_slot, start)
    n_to_y(core_slot).wait_recv()
    own_out(core_slot, start)
    for k in range(1, line):
        if k not in early:
            c_out(k).start()

    def line_source(i):
        low = jnp.minimum(z, line - 1 - z)
        near = i < 2 * low
        distance = jnp.where(near, i // 2 + 1, i + 1 - low)
        below = jnp.where(near, i % 2 == 0, z > low)
        return jnp.where(below, z - distance, z + distance), below

    def line_out(slot, below, act):
        @pl.when(jnp.logical_and(below, z + 1 < line))
        def _():
            act(n_to_up(slot))

        @pl.when(jnp.logical_and(jnp.logical_not(below), z > 0))
        def _():
            act(n_to_down(slot))

    is_end = jnp.logical_or(z == 0, z == line - 1)

    def from_end(zs):
        return jnp.logical_or(zs == 0, zs == line - 1)

    def line_piece(i, cs, act, wait):
        zs, below = line_source(i)
        slot = slot_of(y, zs, cs)
        if wait:
            n_to_y(slot).wait_recv()
        line_out(slot, below, act)
        if cs == 0:

            @pl.when(jnp.logical_not(from_end(zs)))
            def _():
                act(n_to_y(slot))
        else:
            act(n_to_y(slot))

    def crossed_piece(i, act, wait):
        zs, below = line_source(i)

        @pl.when(jnp.logical_and(from_end(zs), jnp.logical_not(is_end)))
        def _():
            slot = slot_of(1 - y, zs, 0)
            if wait:
                n_to_y(slot).wait_recv()
            line_out(slot, below, act)

    def crossed_here(act, wait):
        @pl.when(is_end)
        def _():
            slot = slot_of(1 - y, z, 0)
            if wait:
                n_to_y(slot).wait_recv()
            line_out(slot, z == 0, act)

    def c_direct(k):
        slot = c_in_slot(k, 0)
        c_relay(slot, c_x, x_peer).wait_recv()
        c_relay(slot, c_x, x_peer).start()
        c_relay(slot, c_core, core_peer).start()

    def c_from_core(i, carry):
        slot = 2 * i + 1 - c
        c_relay(slot, c_core, core_peer).wait_recv()
        return carry

    def direct_zero():
        @pl.when(x == 1)
        def _():
            c_direct(0)

    def c_shared(k):
        slot = c_in_slot(k, 1)
        c_relay(slot, c_core, core_peer).wait_recv()
        c_relay(slot, c_core, core_peer).start()

    def shared_zero():
        @pl.when(x == 0)
        def _():
            c_shared(0)

    def gram_rows(i):
        block_tokens = cbuf[...].reshape(tokens, TILE)
        part = slice(i * TILE // 2, (i + 1) * TILE // 2)
        gram_c[part, :] = contract(block_tokens[:, part], block_tokens, 0, 0)

    p = z * 2 + y
    r = p % 4
    edge = jnp.where(jnp.logical_or(r == 0, r == 3), 1, 0)
    block = block_of(p)

    def unit_of(k):
        return edge * (3 * c + k * (1 - 2 * c)) + (1 - edge) * (2 * (r - 1) + c)

    def place_of(k):
        return 4 * block + unit_of(k) - 3 * p

    def strip_columns(place):
        return pl.ds(pl.multiple_of(place * UNIT, UNIT), UNIT)

    def pre_copy(place, send, target):
        view = pre.at[:, strip_columns(place)]
        return remote(view, view, send, pre_recv.at[place], target)

    half = tokens // 2

    def half_rows(h):
        return pl.ds(pl.multiple_of(h * half, half), half)

    def give_copy():
        place = place_of(0) - 3 * (1 - 2 * y)
        return remote(
            give,
            pre.at[half_rows(x), strip_columns(place)],
            pre_send.at[2],
            pre_recv.at[3 + x],
            device(x, 1 - y, z, c),
        )

    outer_place = (r - 1) * 2

    def outer_copy(h, send, target):
        view = pre.at[half_rows(h), strip_columns(outer_place)]
        return remote(view, view, pre_send.at[send], pre_recv.at[3 + h], target)

    def outer_first():
        @pl.when(jnp.logical_and(edge == 0, c == 2 - r))
        def _():
            outer_copy(x, 3, x_peer).wait_recv()
            outer_copy(x, 3, x_peer).start()
            outer_copy(x, 4, core_peer).start()

    def outer_rest():
        @pl.when(jnp.logical_and(edge == 0, c == 2 - r))
        def _():
            outer_copy(1 - x, 5, core_peer).wait_recv()
            outer_copy(1 - x, 5, core_peer).start()

        @pl.when(jnp.logical_and(edge == 0, c == r - 1))
        def _():
            outer_copy(0, 3, core_peer).wait_recv()
            outer_copy(1, 3, core_peer).wait_recv()

    def outer_drain():
        @pl.when(jnp.logical_and(edge == 0, c == 2 - r))
        def _():
            outer_copy(x, 3, x_peer).wait_send()
            outer_copy(x, 4, core_peer).wait_send()
            outer_copy(1 - x, 5, core_peer).wait_send()

    def unit_inverse(k, scale_c):
        unit = unit_of(k)
        first = low_c[:, pl.ds(pl.multiple_of(unit * UNIT, UNIT), UNIT)]
        second = contract(low_c[...], first, 1, 0)
        third = contract(low_c[...], second.astype(jnp.bfloat16), 1, 0)
        row = lax.broadcasted_iota(jnp.int32, (TILE, UNIT), 0)
        column = lax.broadcasted_iota(jnp.int32, (TILE, UNIT), 1) + unit * UNIT
        start4 = jnp.where(row == column, 4.0, 0.0)
        powers = [scale_c, scale_c**2, scale_c**3, scale_c**4]
        inverse = powers[0] * start4 - (6.0 * powers[1]) * first.astype(jnp.float32)
        inverse = inverse + (4.0 * powers[2]) * second - powers[3] * third
        return inverse.astype(jnp.bfloat16)

    def is_mine(k):
        place = place_of(k)
        return jnp.logical_and(place >= 0, place < 3)

    def unit_step(k, scale_c):
        inverse = unit_inverse(k, scale_c)
        inside = is_mine(k)

        @pl.when(inside)
        def _():
            whole = cbuf[...].reshape(tokens, TILE)
            pre[:, strip_columns(place_of(k))] = contract(whole, inverse, 1, 0).astype(jnp.bfloat16)
            pre_copy(place_of(k), pre_send.at[k], core_peer).start()

        @pl.when(jnp.logical_not(inside))
        def _():
            rows = cbuf[pl.ds(x * (groups // 2), groups // 2)].reshape(half, TILE)
            give[...] = contract(rows, inverse, 1, 0).astype(jnp.bfloat16)
            give_copy().start()

    row_slots = pl.ds(y * line * 2, line * 2)
    row_tokens = pl.ds(pl.multiple_of(y * (tokens // 2), tokens // 2), tokens // 2)

    def move(token):
        kind = token[0]
        if kind == "d":
            k = int(token[1])
            if k:
                c_direct(k)
            else:
                direct_zero()
        elif kind == "s":
            k = int(token[1])
            if k:
                c_shared(k)
            else:
                shared_zero()
        elif kind == "L":
            line_piece(int(token[1]), int(token[2]), start, True)
        elif kind == "S":
            crossed_piece(int(token[1]), start, True)
        elif kind == "Y":
            crossed_here(start, True)
        elif kind == "P":
            outer_first()

    def moves(stage):
        @pl.when(is_end)
        def _():
            for token in END[stage]:
                move(token)

        @pl.when(jnp.logical_not(is_end))
        def _():
            for token in MIDDLE[stage]:
                move(token)

    moves(0)
    lax.fori_loop(0, groups // 2, c_from_core, 0)
    local.wait()
    gram_rows(0)
    moves(1)
    gram_rows(1)
    scale_c = rounded_factor(gram_c, low_c, tokens)
    moves(2)
    unit_step(0, scale_c)
    moves(3)

    @pl.when(edge == 1)
    def _():
        unit_step(1, scale_c)

    moves(4)

    def more(i, carry):
        for cs in range(2):
            line_piece(i, cs, start, True)
        crossed_piece(i, start, True)
        return carry

    lax.fori_loop(3, line - 1, more, 0)
    row_n = nbuf[row_slots].reshape(tokens // 2, TILE)
    gram_n[...] = contract(row_n, row_n, 0, 0)
    moves(5)

    def pre_in(place):
        unit = place + 3 * p - 4 * block
        inside = jnp.logical_and(unit >= 0, unit <= 3)
        source = jnp.where(edge == 1, unit // 2, unit - 2 * (r - 1))

        @pl.when(jnp.logical_and(inside, source != c))
        def _():
            pre_copy(place, pre_send.at[0], core_peer).wait_recv()

    for place in range(3):
        pre_in(place)
    outer_rest()

    cross[...] = contract(pre[row_tokens, :], nbuf[row_slots].reshape(tokens // 2, TILE), 0, 0)

    def other_row(i, carry):
        zs, _ = line_source(jnp.maximum(i - 1, 0))
        zs = jnp.where(i == 0, z, zs)
        slot = slot_of(1 - y, zs, 0)

        seen = jnp.where(i == 0, is_end, jnp.logical_and(from_end(zs), jnp.logical_not(is_end)))

        @pl.when(jnp.logical_not(seen))
        def _():
            n_to_y(slot).wait_recv()

        n_to_y(slot + 1).wait_recv()
        piece = nbuf[pl.ds(slot, 2)].reshape(2 * tokens_here, TILE)
        gram_n[...] += contract(piece, piece, 0, 0)
        rows = pl.ds(pl.multiple_of(slot * tokens_here, 2 * tokens_here), 2 * tokens_here)
        cross[...] += contract(pre[rows, :], piece, 0, 0)
        return carry

    lax.fori_loop(0, line, other_row, 0)

    pl.semaphore_signal(meet, inc=1, device_id=x_peer, device_id_type=MESH)
    scale_n = rounded_factor(gram_n, low_n, tokens)

    square = scale_n * scale_n
    first = contract(cross[...].astype(jnp.bfloat16), low_n[...], 1, 0)
    first_low[...] = first.astype(jnp.bfloat16)
    cross[...] = (4.0 * scale_n) * cross[...] - (6.0 * square) * first
    second_low[...] = contract(first_low[...], low_n[...], 1, 0).astype(jnp.bfloat16)

    def result(h):
        rows = pl.ds(pl.multiple_of(h * strip, strip), strip)
        second = second_low[rows, :]
        third = contract(second, low_n[...], 1, 0)
        partial = cross[rows, :] + (4.0 * square * scale_n) * second.astype(jnp.float32)
        return partial - (square * square) * third

    def energy(value):
        total = jnp.sum((value * value).reshape(strip // 8, 8, TILE), axis=0)
        part = total[:, :128]
        for i in range(1, TILE // 128):
            part = part + total[:, i * 128 : (i + 1) * 128]
        return part

    theirs[...] = result(1 - c)
    swap = remote(theirs, arrived, swap_send.at[0], swap_recv.at[0], core_peer)
    swap.start()
    mine[...] = result(c)
    squares[flat] = energy(theirs[...]) + energy(mine[...])

    def sq_copy(d, slot):
        target = (flat + d) % devices
        return remote(
            squares.at[slot],
            squares.at[slot],
            sq_send.at[d],
            sq_recv.at[slot],
            (target // owners, target % owners),
        )

    def sq_start(d, carry):
        sq_copy(d, flat).start()
        return carry

    def sq_wait(d, carry):
        sq_copy(d, (flat + d) % devices).wait_recv()
        sq_copy(d, flat).wait_send()
        return carry

    pl.semaphore_wait(meet, 1)
    lax.fori_loop(1, devices, sq_start, 0)
    n_pass.wait_send()
    own_out(own_slot, drain)
    own_out(core_slot, drain)

    def line_drain(i, carry):
        for cs in range(2):
            line_piece(i, cs, drain, False)
        crossed_piece(i, drain, False)
        return carry

    lax.fori_loop(0, line - 1, line_drain, 0)
    crossed_here(drain, False)
    c_own.wait_send()

    def c_drain(k):
        slot = c_in_slot(k, 0)
        c_out(k).wait_send()
        c_relay(slot, c_x, x_peer).wait_send()
        c_relay(slot, c_core, core_peer).wait_send()

    def c_shared_drain(k):
        c_relay(c_in_slot(k, 1), c_core, core_peer).wait_send()

    for k in range(1, line):
        c_drain(k)
        c_shared_drain(k)

    @pl.when(x == 1)
    def _():
        c_drain(0)

    @pl.when(x == 0)
    def _():
        c_shared_drain(0)

    def unit_drain(k, carry):
        inside = is_mine(k)

        @pl.when(inside)
        def _():
            pre_copy(place_of(k), pre_send.at[k], core_peer).wait_send()

        @pl.when(jnp.logical_not(inside))
        def _():
            give_copy().wait_send()

        return carry

    lax.fori_loop(0, 1 + edge, unit_drain, 0)
    outer_drain()
    swap.wait()
    lax.fori_loop(1, devices, sq_wait, 0)
    total = jnp.sum(squares[...], axis=0)
    total = jnp.sum(jnp.sum(total, axis=0, keepdims=True), axis=1, keepdims=True)
    final = lax.rsqrt(total / (width * out_width) + 1e-06)

    def put(half, value, h):
        put_low[half] = (value * final).astype(jnp.bfloat16)
        columns = pl.ds(pl.multiple_of(h * TILE, TILE), TILE)
        copy = pltpu.make_async_copy(
            put_low.at[half], update_ref.at[:, columns], put_sem.at[half]
        )
        copy.start()
        return copy

    first_put = put(0, mine[...], c)
    second_put = put(1, arrived[...], 1 - c)
    first_put.wait()
    second_put.wait()


def whole(groups, owners, hidden, norm_gain, cotangent):
    tokens_here, width = hidden.shape
    out_width = cotangent.shape[1]
    tokens = groups * tokens_here
    strip = out_width // groups
    line = groups // 4
    low, high = jnp.bfloat16, jnp.float32
    dma = pltpu.SemaphoreType.DMA
    return pl.pallas_call(
        functools.partial(whole_kernel, (groups, owners, tokens_here, width, out_width)),
        out_shape=jax.ShapeDtypeStruct((strip, width // owners), low),
        in_specs=[
            pl.BlockSpec(memory_space=pl.ANY),
            pl.BlockSpec(memory_space=pltpu.VMEM),
            pl.BlockSpec(memory_space=pl.ANY),
        ],
        out_specs=pl.BlockSpec(memory_space=pl.ANY),
        scratch_shapes=[
            pltpu.VMEM((tokens_here, width), low),
            pltpu.VMEM((groups, tokens_here, TILE), low),
            pltpu.VMEM((groups, tokens_here, TILE), low),
            pltpu.VMEM((tokens_here, TILE), low),
            pltpu.VMEM((TILE, TILE), high),
            pltpu.VMEM((TILE, TILE), high),
            pltpu.VMEM((TILE, TILE), low),
            pltpu.VMEM((TILE, TILE), low),
            pltpu.VMEM((tokens, 2 * strip), low),
            pltpu.VMEM((tokens // 2, UNIT), low),
            pltpu.VMEM((2 * strip, TILE), high),
            pltpu.VMEM((2 * strip, TILE), low),
            pltpu.VMEM((2 * strip, TILE), low),
            pltpu.VMEM((strip, TILE), high),
            pltpu.VMEM((strip, TILE), high),
            pltpu.VMEM((strip, TILE), high),
            pltpu.VMEM((groups * owners, 8, 128), high),
            pltpu.VMEM((2, strip, TILE), low),
            dma((2,)),
            pltpu.SemaphoreType.REGULAR,
            dma((2,)),
            dma((line,)),
            dma((groups,)),
            dma((groups,)),
            dma((groups,)),
            dma((1,)),
            dma((groups,)),
            dma((groups,)),
            dma((groups,)),
            dma((groups,)),
            dma((6,)),
            dma((5,)),
            dma((1,)),
            dma((1,)),
            dma((groups * owners,)),
            dma((groups * owners,)),
        ],
        compiler_params=pltpu.CompilerParams(
            collective_id=0, has_side_effects=True, vmem_limit_bytes=60 * 2**20
        ),
    )(hidden, norm_gain.reshape(1, width), cotangent)


def fits(groups, owners, width, out_width):
    line = groups // 4
    return (
        owners == 2
        and width == 2 * owners * TILE
        and groups % 8 == 0
        and line & (line - 1) == 0
        and line >= 4
        and 8 * out_width == 3 * TILE * groups
    )


def step(hidden, norm_gain, cotangent):
    groups, owners = lax.axis_size("dp"), lax.axis_size("owner")
    if fits(groups, owners, hidden.shape[1], cotangent.shape[1]):
        return whole(groups, owners, hidden, norm_gain, cotangent)
    return shards(hidden, norm_gain, cotangent)


def solution(mesh):
    in_specs = (P("dp", None), P(), P("dp", None))
    out_specs = P("dp", "owner")
    return jax.shard_map(step, mesh=mesh, in_specs=in_specs, out_specs=out_specs, check_vma=False)
```
